128 devices in a mesh: seq: 16 (over x, y), cand: 8 (over z, core).
Axes of the slice: x: 4, y: 4, z: 4, core: 2. Of those that a mesh axis runs over, the one named last changes fastest.
Arguments:
- behaviors: float32 [8, 131072, 128], P('cand', 'seq'), may hold values from -15 to 15
- cluster_ids: int32 [8, 131072], P('cand', 'seq'), may hold values from 0 to 2047, as said below
- lengths: int32 [8, 16], P('cand', 'seq'), may hold values from 2048 to 8192
- candidates: bfloat16 [8, 4096, 128], P(None, ('seq', 'cand')), may hold values from -6 to 6
- w_query: bfloat16 [128, 128], replicated, may hold values from -0.5 to 0.5
- w_key: bfloat16 [128, 128], replicated, may hold values from -0.5 to 0.5
- w_hidden: bfloat16 [256, 512], replicated, may hold values from -0.375 to 0.375
- b_hidden: float32 [512], replicated, may hold values from -0.5 to 0.5
- w_out: float32 [512], replicated, may hold values from -0.25 to 0.25
Outputs:
- ranking: float32 [8, 4096], P(None, ('seq', 'cand'))
The draws below stay inside these ranges and needn't reach their ends.
Inputs may be any that keep to these rules, and one draw needn't show every extreme that they name: `cluster_ids`: each user's first 2048 slots name 2048 different clusters.
All inputs are finite; a program needn't handle non-finite values.
Results may differ from the reference program's by a relative error of at most 0.02.
Values may be sent and summed in bfloat16 or wider, within the bound.
A program may use at most 64 MiB of HBM per device.

```python
import jax
import jax.numpy as jnp
from jax import lax

D = 128
C = 2048
H = 512
BEH_DEV = 8192
USERS = 8
HIST = 131072
NC = 4096
N_SEQ = 16


def shared_ids(key):
    base = jax.random.fold_in(key, 7301)
    first_key, second_key, third_key = jax.random.split(base, 3)
    bounds = jax.random.randint(first_key, (USERS, HIST), 1, C + 1)
    ranks = jax.random.randint(second_key, (USERS, HIST), 0, bounds)
    slot = jnp.arange(HIST, dtype=jnp.int32)
    ranks = jnp.where(slot[None, :] < C, slot[None, :], ranks).astype(jnp.int32)
    orders = jax.vmap(lambda k: jax.random.permutation(k, C))(jax.random.split(third_key, USERS)).astype(jnp.int32)
    return jax.vmap(lambda order, rank: order[rank])(orders, ranks).astype(jnp.int32)


def draw_cluster_ids(key, part):
    return shared_ids(key)


def draw_behaviors(key, part):
    ids = shared_ids(key)
    shards = HIST // BEH_DEV
    base = jax.random.fold_in(key, 9157)
    mean_key, drift_key, noise_key = jax.random.split(base, 3)
    means = jnp.clip(2.5 * jax.random.normal(mean_key, (USERS, C, D), jnp.float32), -6.0, 6.0)
    drift = jnp.clip(2.0 * jax.random.normal(drift_key, (USERS, shards * C, D), jnp.float32), -5.0, 5.0)
    noise = jnp.clip(jax.random.normal(noise_key, (USERS, HIST, D), jnp.float32), -4.0, 4.0)
    shard_of = (jnp.arange(HIST, dtype=jnp.int32) // BEH_DEV).astype(jnp.int32)
    drift_index = (shard_of[None, :] * C + ids).astype(jnp.int32)
    picked_means = jax.vmap(lambda table, index: table[index])(means, ids)
    picked_drift = jax.vmap(lambda table, index: table[index])(drift, drift_index)
    return jnp.clip(picked_means + picked_drift + noise, -15.0, 15.0)


def place_ends(result, own_key, smallest, largest):
    shape = result.shape
    place = [jax.random.randint(jax.random.fold_in(own_key, axis), (), 0, shape[axis]) for axis in range(len(shape))]
    result = result.at[tuple(place)].set(smallest)
    longest = shape.index(max(shape))
    place[longest] = (place[longest] + 1) % shape[longest]
    return result.at[tuple(place)].set(largest)


def steps_of(own_key, shape, cuts, least, high):
    def one(dim, parts):
        heights = jax.random.uniform(jax.random.fold_in(jax.random.fold_in(own_key, 6), dim), (parts,), jnp.float32, least / len(cuts), high / len(cuts))
        return jnp.repeat(jnp.exp(heights), shape[dim] // parts).reshape((-1,) + (1,) * (len(shape) - dim - 1))

    factor_of = one(*cuts[0])
    for cut in cuts[1:]:
        factor_of = factor_of * one(*cut)
    return factor_of


def scatter_about(own_key, dims, scale, bound, cuts=(), kind=jnp.bfloat16):
    drawn = scale * jax.random.normal(own_key, dims, jnp.float32)
    if cuts:
        drawn = drawn * steps_of(own_key, dims, cuts, -0.22, 0.18)
    return jnp.clip(drawn, -bound, bound).astype(kind)


def setup_inputs(seed: int = 0) -> dict:
    seeds = jax.random.split(jax.random.key(seed), 10)
    return {
        "behaviors": draw_behaviors(jax.random.fold_in(seeds[9], 71), 0),
        "cluster_ids": draw_cluster_ids(jax.random.fold_in(seeds[9], 71), 0),
        "lengths": place_ends(jax.random.randint(seeds[2], (USERS, N_SEQ), BEH_DEV // 4, BEH_DEV + 1), jax.random.fold_in(seeds[2], 1), BEH_DEV // 4, BEH_DEV).astype(jnp.int32),
        "candidates": scatter_about(seeds[3], (USERS, NC, D), 1.0, 6.0, ((1, 128),)),
        "w_query": scatter_about(seeds[4], (D, D), D ** -0.5, 0.5),
        "w_key": scatter_about(seeds[5], (D, D), D ** -0.5, 0.5),
        "w_hidden": scatter_about(seeds[6], (2 * D, H), (2 * D) ** -0.5, 0.375),
        "b_hidden": jnp.clip(jax.random.uniform(seeds[7], (H,), jnp.float32, -0.5, 0.5), -0.5, 0.5),
        "w_out": scatter_about(seeds[8], (H,), H ** -0.5, 0.25, (), jnp.float32),
    }


def one_user(item_rows, cluster_ids, length_row, cand_rows, w_query, w_key, w_hidden, b_hidden, w_out):
    within = jnp.arange(HIST, dtype=jnp.int32) % BEH_DEV
    limits = jnp.repeat(length_row, BEH_DEV)
    inside = within < limits
    masked = jnp.where(inside[:, None], item_rows, jnp.float32(0.0))
    sums = jax.ops.segment_sum(masked, cluster_ids, num_segments=C)
    counts = jax.ops.segment_sum(inside.astype(jnp.float32), cluster_ids, num_segments=C)
    centroids = (sums / jnp.maximum(counts, 1.0)[:, None]).astype(jnp.bfloat16)
    key_rows = jnp.dot(centroids, w_key, preferred_element_type=jnp.float32).astype(jnp.bfloat16)
    size_bias = jnp.where(counts > 0, jnp.log(1.0 + counts), jnp.float32(-1000000000.0)).astype(jnp.bfloat16)
    queries = jnp.dot(cand_rows, w_query, preferred_element_type=jnp.float32).astype(jnp.bfloat16)
    scores = jnp.dot(queries, key_rows.T, preferred_element_type=jnp.float32) / jnp.sqrt(jnp.float32(D))
    scores = scores + size_bias.astype(jnp.float32)[None, :]
    weights = jax.nn.softmax(scores, axis=-1).astype(jnp.bfloat16)
    attended = jnp.dot(weights, centroids, preferred_element_type=jnp.float32).astype(jnp.bfloat16)
    features = jnp.concatenate([cand_rows, attended], axis=-1)
    hidden = jax.nn.relu(jnp.dot(features, w_hidden, preferred_element_type=jnp.float32) + b_hidden)
    return jnp.dot(hidden, w_out, precision=lax.Precision.HIGHEST)

def reference(behaviors, cluster_ids, lengths, candidates, w_query, w_key, w_hidden, b_hidden, w_out):

    def single(packed):
        item_rows, ids, length_row, cand_rows = packed
        return one_user(item_rows, ids, length_row, cand_rows, w_query, w_key, w_hidden, b_hidden, w_out)
    return lax.map(single, (behaviors, cluster_ids, lengths, candidates))
```

```python
import jax
import jax.numpy as jnp
from jax import lax
from jax.experimental import pallas as pl
from jax.experimental.pallas import tpu as pltpu
from jax.sharding import PartitionSpec as P

BF16 = jnp.bfloat16
F32 = jnp.float32
NX, NY, NCAND = 4, 4, 8
SLOTS, D, HID = 8192, 128, 512
HALF = 1024
CHUNKS = 4
CH = SLOTS // CHUNKS
MB = 256
ROWS = HALF // 16


def remote(src, dst, send, recv, device_id):
    return pltpu.make_async_remote_copy(
        src_ref=src,
        dst_ref=dst,
        send_sem=send,
        recv_sem=recv,
        device_id=device_id,
        device_id_type=pl.DeviceIdType.MESH,
    )


def nt_dot(a, b):
    return lax.dot_general(a, b, (((1,), (1,)), ((), ())), preferred_element_type=F32)


def kernel(
    len_ref,
    beh_ref,
    ids_ref,
    ids2_ref,
    cand_ref,
    wq_ref,
    wk_ref,
    wh_ref,
    bh_ref,
    wo_ref,
    out_ref,
    beh_v,
    rhs,
    rowid,
    acc,
    own,
    s_send,
    rs_buf,
    cnt_send,
    cnt_buf,
    ga,
    gb,
    mine,
    q2,
    wt,
    hc,
    bcol,
    wcol,
    out_send,
    out_buf,
    sc,
    load_sem,
    cand_s,
    cand_r,
    cnt_s,
    cnt_r,
    rs_s,
    rs_r,
    ag_s,
    ag_r,
    out_s,
    out_r,
):
    s = lax.axis_index("seq")
    c = lax.axis_index("cand")
    x, y = s // NY, s % NY

    loads = [
        pltpu.make_async_copy(
            beh_ref.at[0, pl.ds(k * CH, CH), :], beh_v.at[pl.ds(k * CH, CH), :], load_sem.at[k]
        )
        for k in range(CHUNKS)
    ]
    for cp in loads:
        cp.start()

    def seq_at(dx, dy):
        return ((x + dx) % NX) * NY + (y + dy) % NY

    barrier = pltpu.get_barrier_semaphore()
    for k in range(1, 16):
        pl.semaphore_signal(
            barrier, inc=1, device_id=(seq_at(k // 4, k % 4), c), device_id_type=pl.DeviceIdType.MESH
        )
    for j in range(1, NCAND):
        pl.semaphore_signal(
            barrier, inc=1, device_id=(s, (c + j) % NCAND), device_id_type=pl.DeviceIdType.MESH
        )

    length = len_ref[0, 0]
    idrow = ids_ref[...]
    live = lax.broadcasted_iota(jnp.int32, (1, SLOTS), 1) < length
    rowid[...] = jnp.where(live, idrow & (HALF - 1), 4096).astype(F32)
    ahot_row = jnp.where(live, idrow >> 7, 4096).astype(F32)
    ids_t = jnp.concatenate([ids2_ref[...], ids2_ref[...]], axis=0).T

    pl.semaphore_wait(barrier, 22)

    cand_copies = []
    for j in range(1, NCAND):
        peer = (c + j) % NCAND
        cp = remote(cand_ref.at[peer], mine.at[c], cand_s.at[j], cand_r.at[j], (s, peer))
        cp.start()
        cand_copies.append(cp)
    mine[c] = cand_ref[c]

    iota16 = lax.broadcasted_iota(jnp.int32, (MB, 128), 0).astype(F32).astype(BF16)

    def onehot(r0, k0, kc):
        rel = rowid[:, pl.ds(k0, kc)] - r0
        b16 = jnp.broadcast_to(rel, (16, kc)).astype(BF16)
        cols = []
        for t in range(kc // 128):
            bb = jnp.broadcast_to(b16[None, :, t * 128 : (t + 1) * 128], (MB // 16, 16, 128))
            cols.append(jnp.where(iota16 == bb.reshape(MB, 128), BF16(1), BF16(0)))
        return jnp.concatenate(cols, axis=1)

    def block_start(i):
        return (((x + 1 + i) % NX) * MB).astype(F32)

    lane = lax.broadcasted_iota(jnp.int32, (128, 128), 1)
    a_iota = lax.broadcasted_iota(jnp.int32, (16, CH), 0).astype(F32)
    counts = jnp.zeros((16, 128), F32)
    for k in range(CHUNKS):
        loads[k].wait()
        bh = []
        for g in range(k * (CH // 128), (k + 1) * (CH // 128)):
            col = jnp.broadcast_to(ids_t[:, g : g + 1], (128, 128))
            v = beh_v[g * 128 : (g + 1) * 128, :]
            upper = col >= HALF
            rhs[g * 128 : (g + 1) * 128, :128] = jnp.where(upper, 0.0, v).astype(BF16)
            rhs[g * 128 : (g + 1) * 128, 128:] = jnp.where(upper, v, 0.0).astype(BF16)
            bh.append(jnp.where((col & 127) == lane, 1.0, 0.0).astype(BF16))
        ah = jnp.where(
            jnp.broadcast_to(ahot_row[:, k * CH : (k + 1) * CH], (16, CH)) == a_iota, 1.0, 0.0
        ).astype(BF16)
        counts = counts + jnp.dot(ah, jnp.concatenate(bh, axis=0), preferred_element_type=F32)
        part = jnp.dot(
            onehot(block_start(0), k * CH, CH),
            rhs[k * CH : (k + 1) * CH, :],
            preferred_element_type=F32,
        )
        if k == 0:
            acc[...] = part
        else:
            acc[...] += part
    s_send[0] = acc[...].astype(BF16)
    cnt_send[...] = counts

    def rs_copy(i, dy):
        k = ((1 + i) % 4) * 4 + dy
        peer_y = (y + dy) % NY
        return remote(
            s_send.at[i, pl.ds(pl.multiple_of(peer_y * ROWS, ROWS), ROWS), :],
            rs_buf.at[k],
            rs_s.at[k],
            rs_r.at[k],
            (((x + 1 + i) % NX) * NY + peer_y, c),
        )

    def cnt_copy(k):
        return remote(
            cnt_send, cnt_buf.at[k], cnt_s.at[k], cnt_r.at[k], (seq_at(k // 4, k % 4), c)
        )

    for dy in range(4):
        rs_copy(0, dy).start()
    for k in range(1, 16):
        cnt_copy(k).start()

    for cp in cand_copies:
        cp.wait()
    cands = mine[...].reshape(256, 128)
    q = jnp.dot(cands, wq_ref[...], preferred_element_type=F32).astype(BF16)
    q2[...] = nt_dot(q, wk_ref[...]).astype(BF16)
    wt[...] = wh_ref[...].astype(F32).T.astype(BF16)
    bcol[...] = jnp.broadcast_to(bh_ref[...], (128, HID)).T
    wcol[...] = jnp.broadcast_to(wo_ref[...], (128, HID)).T
    hc[...] = nt_dot(wt[:, :D], cands) + jnp.concatenate([bcol[...], bcol[...]], axis=1)

    def block(i):
        return jnp.dot(
            onehot(block_start(i), 0, SLOTS), rhs[...], preferred_element_type=F32
        )

    for i in range(1, 4):
        val = block(i)
        s_send[i] = val.astype(BF16)
        if i < 3:
            for dy in range(4):
                rs_copy(i, dy).start()
        else:
            own[...] = val
            for dy in range(1, 4):
                rs_copy(i, dy).start()

    total = own[pl.ds(pl.multiple_of(y * ROWS, ROWS), ROWS), :]
    for i in range(4):
        for dy in range(4):
            k = ((1 + i) % 4) * 4 + dy
            if k:
                rs_copy(i, dy).wait()
                total = total + rs_buf[k].astype(F32)
    tb = total.astype(BF16)

    def at_rows(ref, px, py):
        return ref.at[pl.ds(pl.multiple_of((px * NY + py) * ROWS, ROWS), ROWS), :]

    at_rows(ga, x, y)[...] = tb[:, :128]
    at_rows(gb, x, y)[...] = tb[:, 128:]

    def ag1(half, d):
        if half == 0:
            blk = at_rows(ga, x, y)
            dev = ((x + d) % NX) * NY + y
        else:
            blk = at_rows(gb, x, y)
            dev = x * NY + (y + d) % NY
        n = half * 16 + d
        return remote(blk, blk, ag_s.at[n], ag_r.at[n], (dev, c))

    def ag2(half, d, e):
        if half == 0:
            blk = at_rows(ga, (x + NX - d) % NX, y)
            dev = x * NY + (y + e) % NY
        else:
            blk = at_rows(gb, x, (y + NY - d) % NY)
            dev = ((x + e) % NX) * NY + y
        n = half * 16 + 4 + d * 3 + e - 1
        return remote(blk, blk, ag_s.at[n], ag_r.at[n], (dev, c))

    order = (1, 3, 2)
    for d in order:
        for half in range(2):
            ag1(half, d).start()
    for d in order:
        for half in range(2):
            ag2(half, 0, d).start()

    for k in range(1, 16):
        cnt_copy(k).wait()
    tot = cnt_send[...]
    for k in range(1, 16):
        tot = tot + cnt_buf[k]
    inv = 1.0 / jnp.maximum(tot, 1.0)
    mult = inv * (1.0 / jnp.sqrt(F32(D)))
    bias = jnp.where(tot > 0, jnp.log(1.0 + tot), F32(-1e9)).astype(BF16).astype(F32)

    for d in order:
        for half in range(2):
            ag1(half, d).wait()
            for e in order:
                ag2(half, d, e).start()
    for d in (0,) + order:
        for half in range(2):
            for e in order:
                ag2(half, d, e).wait()

    gs = (ga, gb)
    mx = jnp.full((256, 128), -jnp.inf, F32)
    for h in range(2):
        raw = nt_dot(q2[...], gs[h][...])
        for j in range(8):
            r = h * 8 + j
            t = raw[:, j * 128 : (j + 1) * 128] * mult[r : r + 1, :] + bias[r : r + 1, :]
            sc[:, r * 128 : (r + 1) * 128] = t
            mx = jnp.maximum(mx, t)
    mx = jnp.broadcast_to(jnp.max(mx, axis=1, keepdims=True), (256, 128))
    den = jnp.zeros((256, 128), F32)
    att = jnp.zeros((256, 128), F32)
    for h in range(2):
        ps = []
        for j in range(8):
            r = h * 8 + j
            e = jnp.exp(sc[:, r * 128 : (r + 1) * 128] - mx)
            den = den + e
            ps.append((e * inv[r : r + 1, :]).astype(BF16))
        att = att + jnp.dot(
            jnp.concatenate(ps, axis=1), gs[h][...], preferred_element_type=F32
        )
    att = (att / jnp.sum(den, axis=1, keepdims=True)).astype(BF16)

    hid = jnp.maximum(hc[...] + nt_dot(wt[:, D:], att), 0.0)
    hid = hid * jnp.concatenate([wcol[...], wcol[...]], axis=1)
    row = jnp.sum(hid, axis=0, keepdims=True)
    for j in range(NCAND):
        out_send[j, :, :32] = row[:, j * 32 : (j + 1) * 32]
    back = []
    for j in range(1, NCAND):
        peer = (c + j) % NCAND
        cp = remote(out_send.at[peer], out_buf.at[c], out_s.at[j], out_r.at[j], (s, peer))
        cp.start()
        back.append(cp)
    out_buf[c] = out_send[c]
    for cp in back:
        cp.wait()
    out_ref[...] = out_buf[:, 0, :32]


def on_device(
    behaviors, cluster_ids, lengths, candidates, w_query, w_key, w_hidden, b_hidden, w_out
):
    vmem = pl.BlockSpec(memory_space=pltpu.VMEM)
    dma = pltpu.SemaphoreType.DMA
    return pl.pallas_call(
        kernel,
        out_shape=jax.ShapeDtypeStruct((8, 32), F32),
        in_specs=[
            pl.BlockSpec(memory_space=pltpu.SMEM),
            pl.BlockSpec(memory_space=pl.ANY),
        ]
        + [vmem] * 8,
        out_specs=vmem,
        scratch_shapes=[
            pltpu.VMEM((SLOTS, D), F32),
            pltpu.VMEM((SLOTS, 2 * D), BF16),
            pltpu.VMEM((1, SLOTS), F32),
            pltpu.VMEM((MB, 2 * D), F32),
            pltpu.VMEM((MB, 2 * D), F32),
            pltpu.VMEM((4, MB, 2 * D), BF16),
            pltpu.VMEM((16, ROWS, 2 * D), BF16),
            pltpu.VMEM((16, 128), F32),
            pltpu.VMEM((16, 16, 128), F32),
            pltpu.VMEM((HALF, D), BF16),
            pltpu.VMEM((HALF, D), BF16),
            pltpu.VMEM((8, 32, D), BF16),
            pltpu.VMEM((256, D), BF16),
            pltpu.VMEM((HID, 2 * D), BF16),
            pltpu.VMEM((HID, 256), F32),
            pltpu.VMEM((HID, 128), F32),
            pltpu.VMEM((HID, 128), F32),
            pltpu.VMEM((8, 1, 128), F32),
            pltpu.VMEM((8, 1, 128), F32),
            pltpu.VMEM((256, 2048), F32),
            dma((CHUNKS,)),
            dma((8,)),
            dma((8,)),
            dma((16,)),
            dma((16,)),
            dma((16,)),
            dma((16,)),
            dma((32,)),
            dma((32,)),
            dma((8,)),
            dma((8,)),
        ],
        compiler_params=pltpu.CompilerParams(collective_id=0, has_side_effects=True),
        name="fused",
    )(
        lengths,
        behaviors,
        cluster_ids,
        cluster_ids.reshape(64, 128),
        candidates,
        w_query,
        w_key,
        w_hidden,
        b_hidden.reshape(1, HID),
        w_out.reshape(1, HID),
    )


def solution(mesh):
    in_specs = (
        P("cand", "seq", None),
        P("cand", "seq"),
        P("cand", "seq"),
        P(None, ("seq", "cand"), None),
        P(),
        P(),
        P(),
        P(),
        P(),
    )
    return jax.shard_map(
        on_device,
        mesh=mesh,
        in_specs=in_specs,
        out_specs=P(None, ("seq", "cand")),
        check_vma=False,
    )
```

```python
import jax
import jax.numpy as jnp
from jax import lax
from jax.experimental import pallas as pl
from jax.experimental.pallas import tpu as pltpu
from jax.sharding import PartitionSpec as P

BF16 = jnp.bfloat16
F32 = jnp.float32
NX, NY, NCAND = 4, 4, 8
SLOTS, D, HID = 8192, 128, 512
HALF = 1024
CHUNKS = 4
CH = SLOTS // CHUNKS
MB = 256
ROWS = HALF // 16


def remote(src, dst, send, recv, device_id):
    return pltpu.make_async_remote_copy(
        src_ref=src,
        dst_ref=dst,
        send_sem=send,
        recv_sem=recv,
        device_id=device_id,
        device_id_type=pl.DeviceIdType.MESH,
    )


def nt_dot(a, b):
    return lax.dot_general(a, b, (((1,), (1,)), ((), ())), preferred_element_type=F32)


SETS = (
    ((2, 2), (1, 2), (3, 2), (2, 3)),
    ((1, 3), (3, 3), (0, 2), (2, 1)),
    ((0, 3), (1, 1), (3, 1), (2, 0)),
    ((0, 0), (1, 0), (3, 0), (0, 1)),
)
ORDER = (1, 3, 2)


def kernel(
    len_hbm,
    beh_hbm,
    ids_hbm,
    ids2_hbm,
    cand_hbm,
    wq_hbm,
    wk_hbm,
    wh_hbm,
    bh_hbm,
    wo_hbm,
    out_ref,
    len_ref,
    beh_v,
    ids_ref,
    ids2_ref,
    cand_ref,
    wq_ref,
    wk_ref,
    wh_ref,
    bh_ref,
    wo_ref,
    rhs,
    rowid,
    acc,
    own,
    s_send,
    rs_buf,
    cnt_x,
    cnt_xb,
    cnt_y,
    cnt_yb,
    ga,
    gb,
    mine,
    q2,
    wt,
    hc,
    bcol,
    wcol,
    out_send,
    out_buf,
    sc,
    load_sem,
    op_sem,
    cand_s,
    cand_r,
    cnt_s,
    cnt_r,
    rs_s,
    rs_r,
    ag_s,
    ag_r,
    out_s,
    out_r,
):
    s = lax.axis_index("seq")
    c = lax.axis_index("cand")
    x, y = s // NY, s % NY

    pairs = (
        (len_hbm, len_ref),
        (ids_hbm, ids_ref),
        (ids2_hbm, ids2_ref),
        (cand_hbm, cand_ref),
        (wq_hbm, wq_ref),
        (wk_hbm, wk_ref),
        (wh_hbm, wh_ref),
        (bh_hbm, bh_ref),
        (wo_hbm, wo_ref),
    )
    ops = [pltpu.make_async_copy(a, b, op_sem.at[n]) for n, (a, b) in enumerate(pairs)]
    loads = [
        pltpu.make_async_copy(
            beh_hbm.at[0, pl.ds(k * CH, CH), :], beh_v.at[pl.ds(k * CH, CH), :], load_sem.at[k]
        )
        for k in range(CHUNKS)
    ]
    for cp in ops[:3] + loads + ops[3:]:
        cp.start()

    def seq_at(dx, dy):
        return ((x + dx) % NX) * NY + (y + dy) % NY

    barrier = pltpu.get_barrier_semaphore()
    for k in range(1, 16):
        pl.semaphore_signal(
            barrier, inc=1, device_id=(seq_at(k // 4, k % 4), c), device_id_type=pl.DeviceIdType.MESH
        )
    for j in range(1, NCAND):
        pl.semaphore_signal(
            barrier, inc=1, device_id=(s, (c + j) % NCAND), device_id_type=pl.DeviceIdType.MESH
        )

    for cp in ops[:3]:
        cp.wait()
    length = len_ref[0, 0]
    idrow = ids_ref[...]
    live = lax.broadcasted_iota(jnp.int32, (1, SLOTS), 1) < length
    rowid[...] = jnp.where(live, idrow & (HALF - 1), 4096).astype(F32)
    ahot_row = jnp.where(live, idrow >> 7, 4096).astype(F32)
    ids_t = jnp.concatenate([ids2_ref[...], ids2_ref[...]], axis=0).T
    half_t = (ids_t >> 10).astype(F32).astype(BF16)
    low_t = (ids_t & 127).astype(F32).astype(BF16)

    iota16 = lax.broadcasted_iota(jnp.int32, (ROWS, 128), 0).astype(F32).astype(BF16)

    def onehot(i, k0, kc):
        parts = []
        for dx, dy in SETS[i]:
            rel = rowid[:, pl.ds(k0, kc)] - (seq_at(dx, dy) * ROWS).astype(F32)
            b16 = jnp.broadcast_to(rel, (16, kc)).astype(BF16)
            cols = []
            for t in range(kc // 128):
                bb = jnp.broadcast_to(b16[None, :, t * 128 : (t + 1) * 128], (ROWS // 16, 16, 128))
                cols.append(jnp.where(iota16 == bb.reshape(ROWS, 128), BF16(1), BF16(0)))
            parts.append(jnp.concatenate(cols, axis=1))
        return jnp.concatenate(parts, axis=0)

    lane = lax.broadcasted_iota(jnp.int32, (128, 128), 1).astype(F32).astype(BF16)
    a_iota = lax.broadcasted_iota(jnp.int32, (16, CH), 0).astype(F32).astype(BF16)
    zero = BF16(0)
    counts = jnp.zeros((16, 128), F32)
    for k in range(CHUNKS):
        loads[k].wait()
        bh = []
        for g in range(k * (CH // 128), (k + 1) * (CH // 128)):
            upper = jnp.broadcast_to(half_t[:, g : g + 1], (128, 128)) != zero
            v = beh_v[g * 128 : (g + 1) * 128, :].astype(BF16)
            rhs[g * 128 : (g + 1) * 128, :128] = jnp.where(upper, zero, v)
            rhs[g * 128 : (g + 1) * 128, 128:] = jnp.where(upper, v, zero)
            low = jnp.broadcast_to(low_t[:, g : g + 1], (128, 128))
            bh.append(jnp.where(low == lane, BF16(1), zero))
        ab = jnp.broadcast_to(ahot_row[:, k * CH : (k + 1) * CH], (16, CH)).astype(BF16)
        ah = jnp.where(ab == a_iota, BF16(1), zero)
        counts = counts + jnp.dot(ah, jnp.concatenate(bh, axis=0), preferred_element_type=F32)
        part = jnp.dot(
            onehot(0, k * CH, CH), rhs[k * CH : (k + 1) * CH, :], preferred_element_type=F32
        )
        if k == 0:
            acc[...] = part
        else:
            acc[...] += part
    s_send[0] = acc[...].astype(BF16)
    cnt_x[...] = counts

    def rs_copy(i, j):
        dx, dy = SETS[i][j]
        k = dx * 4 + dy
        return remote(
            s_send.at[i, pl.ds(j * ROWS, ROWS), :],
            rs_buf.at[k],
            rs_s.at[k],
            rs_r.at[k],
            (seq_at(dx, dy), c),
        )

    def cntx_copy(d):
        return remote(cnt_x, cnt_xb.at[d], cnt_s.at[d], cnt_r.at[d], (seq_at(d, 0), c))

    def cnty_copy(d):
        return remote(cnt_y, cnt_yb.at[d], cnt_s.at[4 + d], cnt_r.at[4 + d], (seq_at(0, d), c))

    ops[3].wait()
    pl.semaphore_wait(barrier, 22)
    for j in range(4):
        rs_copy(0, j).start()
    for d in ORDER:
        cntx_copy(d).start()
    cand_copies = []
    for j in range(1, NCAND):
        peer = (c + j) % NCAND
        cp = remote(cand_ref.at[peer], mine.at[c], cand_s.at[j], cand_r.at[j], (s, peer))
        cp.start()
        cand_copies.append(cp)
    mine[c] = cand_ref[c]

    for i in range(1, 4):
        val = jnp.dot(onehot(i, 0, SLOTS), rhs[...], preferred_element_type=F32)
        s_send[i] = val.astype(BF16)
        if i == 2:
            for d in ORDER:
                cntx_copy(d).wait()
            cnt_y[...] = cnt_x[...] + cnt_xb[1] + cnt_xb[2] + cnt_xb[3]
        if i == 3:
            own[...] = val[:ROWS]
        for j in range(4):
            if SETS[i][j] != (0, 0):
                rs_copy(i, j).start()
        if i == 2:
            for d in ORDER:
                cnty_copy(d).start()

    for cp in ops[4:]:
        cp.wait()
    for cp in cand_copies:
        cp.wait()
    cands = mine[...].reshape(256, 128)
    q = jnp.dot(cands, wq_ref[...], preferred_element_type=F32).astype(BF16)
    q2[...] = nt_dot(q, wk_ref[...]).astype(BF16)
    wt[...] = wh_ref[...].astype(F32).T.astype(BF16)
    bcol[...] = jnp.broadcast_to(bh_ref[...], (128, HID)).T
    wcol[...] = jnp.broadcast_to(wo_ref[...], (128, HID)).T
    hc[...] = nt_dot(wt[:, :D], cands) + jnp.concatenate([bcol[...], bcol[...]], axis=1)
    for d in ORDER:
        cnty_copy(d).wait()
    tot = cnt_y[...] + cnt_yb[1] + cnt_yb[2] + cnt_yb[3]
    inv = 1.0 / jnp.maximum(tot, 1.0)
    mult = inv * (1.0 / jnp.sqrt(F32(D)))
    bias = jnp.where(tot > 0, jnp.log(1.0 + tot), F32(-1e9)).astype(BF16).astype(F32)

    total = own[...]
    for i in range(4):
        for j in range(4):
            dx, dy = SETS[i][j]
            if (dx, dy) != (0, 0):
                rs_copy(i, j).wait()
                total = total + rs_buf[dx * 4 + dy].astype(F32)
    tb = total.astype(BF16)

    def at_rows(ref, px, py):
        return ref.at[pl.ds(pl.multiple_of((px * NY + py) * ROWS, ROWS), ROWS), :]

    at_rows(ga, x, y)[...] = tb[:, :128]
    at_rows(gb, x, y)[...] = tb[:, 128:]

    def ag1(half, d):
        blk = at_rows((ga, gb)[half], x, y)
        dev = seq_at(d, 0) if half == 0 else seq_at(0, d)
        n = half * 16 + d
        return remote(blk, blk, ag_s.at[n], ag_r.at[n], (dev, c))

    def ag2(half, d, e):
        n = half * 16 + 4 + d * 3 + e - 1
        if (d, e) == (2, 2):
            blk = at_rows((ga, gb)[half], x, y)
            dev = seq_at(2, 2)
        elif half == 0:
            blk = at_rows(ga, (x + NX - d) % NX, y)
            dev = seq_at(0, e)
        else:
            blk = at_rows(gb, x, (y + NY - d) % NY)
            dev = seq_at(e, 0)
        return remote(blk, blk, ag_s.at[n], ag_r.at[n], (dev, c))

    for d in ORDER:
        for half in range(2):
            ag1(half, d).start()
    for half in range(2):
        ag2(half, 2, 2).start()
    for d in (2, 1, 3):
        for half in range(2):
            ag2(half, 0, d).start()
    for d in ORDER:
        for half in range(2):
            ag1(half, d).wait()
            for e in (2, 1, 3):
                if (d, e) != (2, 2):
                    ag2(half, d, e).start()
    for d in (0,) + ORDER:
        for half in range(2):
            for e in ORDER:
                ag2(half, d, e).wait()

    gs = (ga, gb)
    mx = jnp.full((256, 128), -jnp.inf, F32)
    for h in range(2):
        raw = nt_dot(q2[...], gs[h][...])
        for j in range(8):
            r = h * 8 + j
            t = raw[:, j * 128 : (j + 1) * 128] * mult[r : r + 1, :] + bias[r : r + 1, :]
            sc[:, r * 128 : (r + 1) * 128] = t
            mx = jnp.maximum(mx, t)
    mx = jnp.broadcast_to(jnp.max(mx, axis=1, keepdims=True), (256, 128))
    den = jnp.zeros((256, 128), F32)
    att = jnp.zeros((256, 128), F32)
    for h in range(2):
        ps = []
        for j in range(8):
            r = h * 8 + j
            e = jnp.exp(sc[:, r * 128 : (r + 1) * 128] - mx)
            den = den + e
            ps.append((e * inv[r : r + 1, :]).astype(BF16))
        att = att + jnp.dot(
            jnp.concatenate(ps, axis=1), gs[h][...], preferred_element_type=F32
        )
    att = (att / jnp.sum(den, axis=1, keepdims=True)).astype(BF16)

    hid = jnp.maximum(hc[...] + nt_dot(wt[:, D:], att), 0.0)
    hid = hid * jnp.concatenate([wcol[...], wcol[...]], axis=1)
    row = jnp.sum(hid, axis=0, keepdims=True)
    for j in range(NCAND):
        out_send[j, :, :32] = row[:, j * 32 : (j + 1) * 32]
    back = []
    for j in range(1, NCAND):
        peer = (c + j) % NCAND
        cp = remote(out_send.at[peer], out_buf.at[c], out_s.at[j], out_r.at[j], (s, peer))
        cp.start()
        back.append(cp)
    out_buf[c] = out_send[c]
    for cp in back:
        cp.wait()
    out_ref[...] = out_buf[:, 0, :32]


def on_device(
    behaviors, cluster_ids, lengths, candidates, w_query, w_key, w_hidden, b_hidden, w_out
):
    vmem = pl.BlockSpec(memory_space=pltpu.VMEM)
    dma = pltpu.SemaphoreType.DMA
    return pl.pallas_call(
        kernel,
        out_shape=jax.ShapeDtypeStruct((8, 32), F32),
        in_specs=[pl.BlockSpec(memory_space=pltpu.HBM)] * 10,
        out_specs=vmem,
        scratch_shapes=[
            pltpu.SMEM((1, 1), jnp.int32),
            pltpu.VMEM((SLOTS, D), F32),
            pltpu.VMEM((1, SLOTS), jnp.int32),
            pltpu.VMEM((64, 128), jnp.int32),
            pltpu.VMEM((8, 32, D), BF16),
            pltpu.VMEM((D, D), BF16),
            pltpu.VMEM((D, D), BF16),
            pltpu.VMEM((2 * D, HID), BF16),
            pltpu.VMEM((1, HID), F32),
            pltpu.VMEM((1, HID), F32),
            pltpu.VMEM((SLOTS, 2 * D), BF16),
            pltpu.VMEM((1, SLOTS), F32),
            pltpu.VMEM((MB, 2 * D), F32),
            pltpu.VMEM((ROWS, 2 * D), F32),
            pltpu.VMEM((4, MB, 2 * D), BF16),
            pltpu.VMEM((16, ROWS, 2 * D), BF16),
            pltpu.VMEM((16, 128), F32),
            pltpu.VMEM((4, 16, 128), F32),
            pltpu.VMEM((16, 128), F32),
            pltpu.VMEM((4, 16, 128), F32),
            pltpu.VMEM((HALF, D), BF16),
            pltpu.VMEM((HALF, D), BF16),
            pltpu.VMEM((8, 32, D), BF16),
            pltpu.VMEM((256, D), BF16),
            pltpu.VMEM((HID, 2 * D), BF16),
            pltpu.VMEM((HID, 256), F32),
            pltpu.VMEM((HID, 128), F32),
            pltpu.VMEM((HID, 128), F32),
            pltpu.VMEM((8, 1, 128), F32),
            pltpu.VMEM((8, 1, 128), F32),
            pltpu.VMEM((256, 2048), F32),
            dma((CHUNKS,)),
            dma((9,)),
            dma((8,)),
            dma((8,)),
            dma((8,)),
            dma((8,)),
            dma((16,)),
            dma((16,)),
            dma((32,)),
            dma((32,)),
            dma((8,)),
            dma((8,)),
        ],
        compiler_params=pltpu.CompilerParams(collective_id=0, has_side_effects=True),
        name="fused",
    )(
        lengths,
        behaviors,
        cluster_ids,
        cluster_ids.reshape(64, 128),
        candidates,
        w_query,
        w_key,
        w_hidden,
        b_hidden.reshape(1, HID),
        w_out.reshape(1, HID),
    )


def solution(mesh):
    in_specs = (
        P("cand", "seq", None),
        P("cand", "seq"),
        P("cand", "seq"),
        P(None, ("seq", "cand"), None),
        P(),
        P(),
        P(),
        P(),
        P(),
    )
    return jax.shard_map(
        on_device,
        mesh=mesh,
        in_specs=in_specs,
        out_specs=P(None, ("seq", "cand")),
        check_vma=False,
    )
```

```python
import jax
import jax.numpy as jnp
from jax import lax
from jax.experimental import pallas as pl
from jax.experimental.pallas import tpu as pltpu
from jax.sharding import PartitionSpec as P

BF16 = jnp.bfloat16
F32 = jnp.float32
NX, NY, NCAND = 4, 4, 8
SLOTS, D, HID = 8192, 128, 512
HALF = 1024
CHUNKS = 4
CH = SLOTS // CHUNKS
MB = 256
ROWS = HALF // 16


def remote(src, dst, send, recv, device_id):
    return pltpu.make_async_remote_copy(
        src_ref=src,
        dst_ref=dst,
        send_sem=send,
        recv_sem=recv,
        device_id=device_id,
        device_id_type=pl.DeviceIdType.MESH,
    )


def nt_dot(a, b):
    return lax.dot_general(a, b, (((1,), (1,)), ((), ())), preferred_element_type=F32)


SETS = (
    ((2, 2), (1, 2), (3, 2), (2, 3)),
    ((1, 3), (3, 3), (0, 2), (2, 1)),
    ((0, 3), (1, 1), (3, 1), (2, 0)),
    ((0, 0), (1, 0), (3, 0), (0, 1)),
)
ORDER = (1, 3, 2)


def kernel(
    len_hbm,
    beh_hbm,
    ids_hbm,
    ids2_hbm,
    cand_hbm,
    wq_hbm,
    wk_hbm,
    wh_hbm,
    bh_hbm,
    wo_hbm,
    out_ref,
    len_ref,
    beh_v,
    ids_ref,
    ids2_ref,
    cand_ref,
    wq_ref,
    wk_ref,
    wh_ref,
    bh_ref,
    wo_ref,
    rhs,
    own16,
    low16,
    acc,
    own,
    s_send,
    rs_buf,
    cnt_x,
    cnt_xb,
    cnt_y,
    cnt_yb,
    ga,
    gb,
    mine,
    q2,
    wt,
    hc,
    bcol,
    wcol,
    out_send,
    out_buf,
    inv_ref,
    mult_ref,
    bias_ref,
    sc,
    load_sem,
    op_sem,
    cand_s,
    cand_r,
    cnt_s,
    cnt_r,
    rs_s,
    rs_r,
    ag_s,
    ag_r,
    out_s,
    out_r,
):
    s = lax.axis_index("seq")
    c = lax.axis_index("cand")
    x, y = s // NY, s % NY

    pairs = (
        (len_hbm, len_ref),
        (ids_hbm, ids_ref),
        (ids2_hbm, ids2_ref),
        (cand_hbm, cand_ref),
        (wq_hbm, wq_ref),
        (wk_hbm, wk_ref),
        (wh_hbm, wh_ref),
        (bh_hbm, bh_ref),
        (wo_hbm, wo_ref),
    )
    ops = [pltpu.make_async_copy(a, b, op_sem.at[n]) for n, (a, b) in enumerate(pairs)]
    loads = [
        pltpu.make_async_copy(
            beh_hbm.at[0, pl.ds(k * CH, CH), :], beh_v.at[pl.ds(k * CH, CH), :], load_sem.at[k]
        )
        for k in range(CHUNKS)
    ]
    for cp in ops[:3] + loads + ops[3:]:
        cp.start()

    def seq_at(dx, dy):
        return ((x + dx) % NX) * NY + (y + dy) % NY

    barrier = pltpu.get_barrier_semaphore()
    for k in range(1, 16):
        pl.semaphore_signal(
            barrier, inc=1, device_id=(seq_at(k // 4, k % 4), c), device_id_type=pl.DeviceIdType.MESH
        )
    for j in range(1, NCAND):
        pl.semaphore_signal(
            barrier, inc=1, device_id=(s, (c + j) % NCAND), device_id_type=pl.DeviceIdType.MESH
        )

    for cp in ops[:3]:
        cp.wait()
    length = len_ref[0, 0]
    idrow = ids_ref[...]
    live = lax.broadcasted_iota(jnp.int32, (1, SLOTS), 1) < length
    high = (idrow >> 8) & 3
    mid = (idrow >> 6) & 3
    owner_row = jnp.where(idrow >= HALF, mid * 4 + high, high * 4 + mid)
    low_row = jnp.where(live, idrow & (ROWS - 1), 255)
    own16[...] = jnp.broadcast_to(owner_row.astype(F32), (16, SLOTS)).astype(BF16)
    low16[...] = jnp.broadcast_to(low_row.astype(F32), (16, SLOTS)).astype(BF16)
    ahot_row = jnp.where(live, idrow >> 7, 255).astype(F32)
    ids_t = jnp.concatenate([ids2_ref[...], ids2_ref[...]], axis=0).T
    half_t = (ids_t >> 10).astype(F32).astype(BF16)
    low_t = (ids_t & 127).astype(F32).astype(BF16)

    iota16 = lax.broadcasted_iota(jnp.int32, (ROWS, 128), 0).astype(F32).astype(BF16)

    def onehot(i, k0, kc):
        parts = []
        for dx, dy in SETS[i]:
            p16 = jnp.full((16, kc), seq_at(dx, dy).astype(F32), F32).astype(BF16)
            b16 = jnp.where(own16[:, pl.ds(k0, kc)] == p16, low16[:, pl.ds(k0, kc)], BF16(255))
            cols = []
            for t in range(kc // 128):
                bb = jnp.broadcast_to(b16[None, :, t * 128 : (t + 1) * 128], (ROWS // 16, 16, 128))
                cols.append(jnp.where(iota16 == bb.reshape(ROWS, 128), BF16(1), BF16(0)))
            parts.append(jnp.concatenate(cols, axis=1))
        return jnp.concatenate(parts, axis=0)

    lane = lax.broadcasted_iota(jnp.int32, (128, 128), 1).astype(F32).astype(BF16)
    a_iota = lax.broadcasted_iota(jnp.int32, (16, CH), 0).astype(F32).astype(BF16)
    zero = BF16(0)
    counts = jnp.zeros((16, 128), F32)
    for k in range(CHUNKS):
        loads[k].wait()
        bh = []
        for g in range(k * (CH // 128), (k + 1) * (CH // 128)):
            upper = jnp.broadcast_to(half_t[:, g : g + 1], (128, 128)) != zero
            v = beh_v[g * 128 : (g + 1) * 128, :].astype(BF16)
            rhs[g * 128 : (g + 1) * 128, :128] = jnp.where(upper, zero, v)
            rhs[g * 128 : (g + 1) * 128, 128:] = jnp.where(upper, v, zero)
            low = jnp.broadcast_to(low_t[:, g : g + 1], (128, 128))
            bh.append(jnp.where(low == lane, BF16(1), zero))
        ab = jnp.broadcast_to(ahot_row[:, k * CH : (k + 1) * CH], (16, CH)).astype(BF16)
        ah = jnp.where(ab == a_iota, BF16(1), zero)
        counts = counts + jnp.dot(ah, jnp.concatenate(bh, axis=0), preferred_element_type=F32)
        part = jnp.dot(
            onehot(0, k * CH, CH), rhs[k * CH : (k + 1) * CH, :], preferred_element_type=F32
        )
        if k == 0:
            acc[...] = part
        else:
            acc[...] += part
    s_send[0] = acc[...].astype(BF16)
    cnt_x[...] = counts

    def rs_copy(i, j):
        dx, dy = SETS[i][j]
        k = dx * 4 + dy
        return remote(
            s_send.at[i, pl.ds(j * ROWS, ROWS), :],
            rs_buf.at[k],
            rs_s.at[k],
            rs_r.at[k],
            (seq_at(dx, dy), c),
        )

    def cntx_copy(d):
        return remote(cnt_x, cnt_xb.at[d], cnt_s.at[d], cnt_r.at[d], (seq_at(d, 0), c))

    def cnty_copy(d):
        return remote(cnt_y, cnt_yb.at[d], cnt_s.at[4 + d], cnt_r.at[4 + d], (seq_at(0, d), c))

    ops[3].wait()
    pl.semaphore_wait(barrier, 22)
    for j in range(4):
        rs_copy(0, j).start()
    for d in ORDER:
        cntx_copy(d).start()
    cand_copies = []
    for j in range(1, NCAND):
        peer = (c + j) % NCAND
        cp = remote(cand_ref.at[peer], mine.at[c], cand_s.at[j], cand_r.at[j], (s, peer))
        cp.start()
        cand_copies.append(cp)
    mine[c] = cand_ref[c]

    for i in range(1, 4):
        val = jnp.dot(onehot(i, 0, SLOTS), rhs[...], preferred_element_type=F32)
        s_send[i] = val.astype(BF16)
        if i == 2:
            for d in ORDER:
                cntx_copy(d).wait()
            cnt_y[...] = cnt_x[...] + cnt_xb[1] + cnt_xb[2] + cnt_xb[3]
        if i == 3:
            own[...] = val[:ROWS]
        for j in range(4):
            if SETS[i][j] != (0, 0):
                rs_copy(i, j).start()
        if i == 2:
            for d in ORDER:
                cnty_copy(d).start()

    for cp in ops[4:]:
        cp.wait()
    for cp in cand_copies:
        cp.wait()
    cands = mine[...].reshape(256, 128)
    q = jnp.dot(cands, wq_ref[...], preferred_element_type=F32).astype(BF16)
    q2[...] = nt_dot(q, wk_ref[...]).astype(BF16)
    wt[...] = wh_ref[...].astype(F32).T.astype(BF16)
    bcol[...] = jnp.broadcast_to(bh_ref[...], (128, HID)).T
    wcol[...] = jnp.broadcast_to(wo_ref[...], (128, HID)).T
    hc[...] = nt_dot(wt[:, :D], cands) + jnp.concatenate([bcol[...], bcol[...]], axis=1)
    for d in ORDER:
        cnty_copy(d).wait()
    tot = cnt_y[...] + cnt_yb[1] + cnt_yb[2] + cnt_yb[3]
    inv = 1.0 / jnp.maximum(tot, 1.0)
    inv_ref[...] = inv
    mult_ref[...] = inv * (1.0 / jnp.sqrt(F32(D)))
    bias_ref[...] = (
        jnp.where(tot > 0, jnp.log(1.0 + tot), F32(-1e9)).astype(BF16).astype(F32)
    )

    total = own[...]
    for i in range(4):
        for j in range(4):
            dx, dy = SETS[i][j]
            if (dx, dy) != (0, 0):
                rs_copy(i, j).wait()
                total = total + rs_buf[dx * 4 + dy].astype(F32)
    tb = total.astype(BF16)

    gs = (ga, gb)

    def at_rows(half, px, py):
        p = py * NX + px if half else px * NY + py
        return gs[half].at[pl.ds(pl.multiple_of(p * ROWS, ROWS), ROWS), :]

    at_rows(0, x, y)[...] = tb[:, :128]
    at_rows(1, x, y)[...] = tb[:, 128:]

    def ag1(half, d):
        blk = at_rows(half, x, y)
        dev = seq_at(0, d) if half else seq_at(d, 0)
        n = half * 16 + d
        return remote(blk, blk, ag_s.at[n], ag_r.at[n], (dev, c))

    def ag2(half, d, e):
        n = half * 16 + 4 + d * 3 + e - 1
        if (d, e) == (2, 2):
            blk = at_rows(half, x, y)
            dev = seq_at(2, 2)
        elif half == 0:
            blk = at_rows(0, (x + NX - d) % NX, y)
            dev = seq_at(0, e)
        else:
            blk = at_rows(1, x, (y + NY - d) % NY)
            dev = seq_at(e, 0)
        return remote(blk, blk, ag_s.at[n], ag_r.at[n], (dev, c))

    for d in ORDER:
        for half in range(2):
            ag1(half, d).start()
    for half in range(2):
        ag2(half, 2, 2).start()
    for d in (2, 1, 3):
        for half in range(2):
            ag2(half, 0, d).start()
    for d in ORDER:
        for half in range(2):
            ag1(half, d).wait()
            for e in (2, 1, 3):
                if (d, e) != (2, 2):
                    ag2(half, d, e).start()

    top = den = att = None
    for dists in ((0,), (1, 3), (2,)):
        keys, rows = [], []
        for d in dists:
            for half in range(2):
                for e in ORDER:
                    ag2(half, d, e).wait()
                g = (y + NY - d) % NY if half else (x + NX - d) % NX
                keys.append(gs[half][pl.ds(pl.multiple_of(g * MB, MB), MB), :])
                rows += [half * 8 + g * 2, half * 8 + g * 2 + 1]
        new = None
        for n, kb in enumerate(keys):
            raw = nt_dot(q2[...], kb)
            for j in range(2):
                r = rows[2 * n + j]
                t = raw[:, j * 128 : (j + 1) * 128] * mult_ref[pl.ds(r, 1), :]
                t = t + bias_ref[pl.ds(r, 1), :]
                sc[:, (2 * n + j) * 128 : (2 * n + j + 1) * 128] = t
                new = t if new is None else jnp.maximum(new, t)
        new = jnp.broadcast_to(jnp.max(new, axis=1, keepdims=True), (256, 128))
        if top is not None:
            new = jnp.maximum(top, new)
            alpha = jnp.exp(top - new)
            den = den * alpha
            att = att * alpha
        top = new
        for n, kb in enumerate(keys):
            ps = []
            for j in range(2):
                r = rows[2 * n + j]
                e = jnp.exp(sc[:, (2 * n + j) * 128 : (2 * n + j + 1) * 128] - top)
                den = e if den is None else den + e
                ps.append((e * inv_ref[pl.ds(r, 1), :]).astype(BF16))
            pv = jnp.dot(jnp.concatenate(ps, axis=1), kb, preferred_element_type=F32)
            att = pv if att is None else att + pv
    att = (att / jnp.sum(den, axis=1, keepdims=True)).astype(BF16)

    hid = jnp.maximum(hc[...] + nt_dot(wt[:, D:], att), 0.0)
    hid = hid * jnp.concatenate([wcol[...], wcol[...]], axis=1)
    row = jnp.sum(hid, axis=0, keepdims=True)
    for j in range(NCAND):
        out_send[j, :, :32] = row[:, j * 32 : (j + 1) * 32]
    back = []
    for j in range(1, NCAND):
        peer = (c + j) % NCAND
        cp = remote(out_send.at[peer], out_buf.at[c], out_s.at[j], out_r.at[j], (s, peer))
        cp.start()
        back.append(cp)
    out_buf[c] = out_send[c]
    for cp in back:
        cp.wait()
    out_ref[...] = out_buf[:, 0, :32]


def on_device(
    behaviors, cluster_ids, lengths, candidates, w_query, w_key, w_hidden, b_hidden, w_out
):
    vmem = pl.BlockSpec(memory_space=pltpu.VMEM)
    dma = pltpu.SemaphoreType.DMA
    return pl.pallas_call(
        kernel,
        out_shape=pltpu.VMEM((8, 32), F32),
        in_specs=[pl.BlockSpec(memory_space=pltpu.HBM)] * 10,
        out_specs=vmem,
        scratch_shapes=[
            pltpu.SMEM((1, 1), jnp.int32),
            pltpu.VMEM((SLOTS, D), F32),
            pltpu.VMEM((1, SLOTS), jnp.int32),
            pltpu.VMEM((64, 128), jnp.int32),
            pltpu.VMEM((8, 32, D), BF16),
            pltpu.VMEM((D, D), BF16),
            pltpu.VMEM((D, D), BF16),
            pltpu.VMEM((2 * D, HID), BF16),
            pltpu.VMEM((1, HID), F32),
            pltpu.VMEM((1, HID), F32),
            pltpu.VMEM((SLOTS, 2 * D), BF16),
            pltpu.VMEM((16, SLOTS), BF16),
            pltpu.VMEM((16, SLOTS), BF16),
            pltpu.VMEM((MB, 2 * D), F32),
            pltpu.VMEM((ROWS, 2 * D), F32),
            pltpu.VMEM((4, MB, 2 * D), BF16),
            pltpu.VMEM((16, ROWS, 2 * D), BF16),
            pltpu.VMEM((16, 128), F32),
            pltpu.VMEM((4, 16, 128), F32),
            pltpu.VMEM((16, 128), F32),
            pltpu.VMEM((4, 16, 128), F32),
            pltpu.VMEM((HALF, D), BF16),
            pltpu.VMEM((HALF, D), BF16),
            pltpu.VMEM((8, 32, D), BF16),
            pltpu.VMEM((256, D), BF16),
            pltpu.VMEM((HID, 2 * D), BF16),
            pltpu.VMEM((HID, 256), F32),
            pltpu.VMEM((HID, 128), F32),
            pltpu.VMEM((HID, 128), F32),
            pltpu.VMEM((8, 1, 128), F32),
            pltpu.VMEM((8, 1, 128), F32),
            pltpu.VMEM((16, 128), F32),
            pltpu.VMEM((16, 128), F32),
            pltpu.VMEM((16, 128), F32),
            pltpu.VMEM((256, 1024), F32),
            dma((CHUNKS,)),
            dma((9,)),
            dma((8,)),
            dma((8,)),
            dma((8,)),
            dma((8,)),
            dma((16,)),
            dma((16,)),
            dma((32,)),
            dma((32,)),
            dma((8,)),
            dma((8,)),
        ],
        compiler_params=pltpu.CompilerParams(collective_id=0, has_side_effects=True),
        name="fused",
    )(
        lengths,
        behaviors,
        cluster_ids,
        cluster_ids.reshape(64, 128),
        candidates,
        w_query,
        w_key,
        w_hidden,
        b_hidden.reshape(1, HID),
        w_out.reshape(1, HID),
    )


def solution(mesh):
    in_specs = (
        P("cand", "seq", None),
        P("cand", "seq"),
        P("cand", "seq"),
        P(None, ("seq", "cand"), None),
        P(),
        P(),
        P(),
        P(),
        P(),
    )
    return jax.shard_map(
        on_device,
        mesh=mesh,
        in_specs=in_specs,
        out_specs=P(None, ("seq", "cand")),
        check_vma=False,
    )
```

```python
import jax
import jax.numpy as jnp
from jax import lax
from jax.experimental import pallas as pl
from jax.experimental.pallas import tpu as pltpu
from jax.sharding import PartitionSpec as P

BF16 = jnp.bfloat16
F32 = jnp.float32
NX, NY, NCAND = 4, 4, 8
SLOTS, D, HID = 8192, 128, 512
HALF = 1024
CHUNKS = 4
CH = SLOTS // CHUNKS
MB = 256
ROWS = HALF // 16


def remote(src, dst, send, recv, device_id):
    return pltpu.make_async_remote_copy(
        src_ref=src,
        dst_ref=dst,
        send_sem=send,
        recv_sem=recv,
        device_id=device_id,
        device_id_type=pl.DeviceIdType.MESH,
    )


def wait_bytes(ref, sem):
    pltpu.make_async_copy(ref, ref, sem).wait()


def nt_dot(a, b):
    return lax.dot_general(a, b, (((1,), (1,)), ((), ())), preferred_element_type=F32)


SETS = (
    ((2, 2), (1, 2), (3, 2), (2, 3)),
    ((1, 3), (3, 3), (0, 2), (2, 1)),
    ((0, 3), (1, 1), (3, 1), (2, 0)),
    ((0, 0), (1, 0), (3, 0), (0, 1)),
)
ORDER = (1, 3, 2)


def kernel(
    len_hbm,
    beh_hbm,
    ids_hbm,
    ids2_hbm,
    cand_hbm,
    wq_hbm,
    wk_hbm,
    wh_hbm,
    bh_hbm,
    wo_hbm,
    out_ref,
    len_ref,
    beh_v,
    ids_ref,
    ids2_ref,
    cand_ref,
    wq_ref,
    wk_ref,
    wh_ref,
    bh_ref,
    wo_ref,
    rhs,
    own16,
    low16,
    acc,
    own,
    s_send,
    rs_buf,
    cnt_x,
    cnt_xb,
    cnt_y,
    cnt_yb,
    ga,
    gb,
    mine,
    q2,
    wt,
    hc,
    bcol,
    wcol,
    out_send,
    out_buf,
    inv_ref,
    mult_ref,
    bias_ref,
    sc,
    load_sem,
    op_sem,
    cand_s,
    cnt_s,
    cnt_r,
    rs_s,
    rs_r,
    ag_s,
    ag_r,
    out_s,
):
    s = lax.axis_index("seq")
    c = lax.axis_index("cand")
    x, y = s // NY, s % NY

    pairs = (
        (len_hbm, len_ref),
        (ids_hbm, ids_ref),
        (ids2_hbm, ids2_ref),
        (cand_hbm, cand_ref),
        (wq_hbm, wq_ref),
        (wk_hbm, wk_ref),
        (wh_hbm, wh_ref),
        (bh_hbm, bh_ref),
        (wo_hbm, wo_ref),
    )
    ops = [pltpu.make_async_copy(a, b, op_sem.at[n]) for n, (a, b) in enumerate(pairs)]
    loads = [
        pltpu.make_async_copy(
            beh_hbm.at[0, pl.ds(k * CH, CH), :], beh_v.at[pl.ds(k * CH, CH), :], load_sem.at[k]
        )
        for k in range(CHUNKS)
    ]
    for cp in ops[:3] + loads + ops[3:]:
        cp.start()

    def seq_at(dx, dy):
        return ((x + dx) % NX) * NY + (y + dy) % NY

    barrier = pltpu.get_barrier_semaphore()
    for k in range(1, 16):
        pl.semaphore_signal(
            barrier, inc=1, device_id=(seq_at(k // 4, k % 4), c), device_id_type=pl.DeviceIdType.MESH
        )
    for j in range(1, NCAND):
        pl.semaphore_signal(
            barrier, inc=1, device_id=(s, (c + j) % NCAND), device_id_type=pl.DeviceIdType.MESH
        )

    for cp in ops[:3]:
        cp.wait()
    length = len_ref[0, 0]
    idrow = ids_ref[...]
    live = lax.broadcasted_iota(jnp.int32, (1, SLOTS), 1) < length
    high = (idrow >> 8) & 3
    mid = (idrow >> 6) & 3
    owner_row = jnp.where(idrow >= HALF, mid * 4 + high, high * 4 + mid)
    low_row = jnp.where(live, idrow & (ROWS - 1), 255)
    own16[...] = jnp.broadcast_to(owner_row.astype(F32), (16, SLOTS)).astype(BF16)
    low16[...] = jnp.broadcast_to(low_row.astype(F32), (16, SLOTS)).astype(BF16)
    ahot_row = jnp.where(live, idrow >> 7, 255).astype(F32)
    ids_t = jnp.concatenate([ids2_ref[...], ids2_ref[...]], axis=0).T
    half_t = (ids_t >> 10).astype(F32).astype(BF16)
    low_t = (ids_t & 127).astype(F32).astype(BF16)

    iota16 = lax.broadcasted_iota(jnp.int32, (ROWS, 128), 0).astype(F32).astype(BF16)

    def onehot(owners, k0, kc):
        parts = []
        for dx, dy in owners:
            p16 = jnp.full((16, kc), seq_at(dx, dy).astype(F32), F32).astype(BF16)
            b16 = jnp.where(own16[:, pl.ds(k0, kc)] == p16, low16[:, pl.ds(k0, kc)], BF16(255))
            cols = []
            for t in range(kc // 128):
                bb = jnp.broadcast_to(b16[None, :, t * 128 : (t + 1) * 128], (ROWS // 16, 16, 128))
                cols.append(jnp.where(iota16 == bb.reshape(ROWS, 128), BF16(1), BF16(0)))
            parts.append(jnp.concatenate(cols, axis=1))
        return jnp.concatenate(parts, axis=0)

    def block_sums(i, k0, kc):
        return [
            jnp.dot(onehot(owners, k0, kc), rhs[k0 : k0 + kc, :], preferred_element_type=F32)
            for owners in (SETS[i][:2], SETS[i][2:])
        ]

    lane = lax.broadcasted_iota(jnp.int32, (128, 128), 1).astype(F32).astype(BF16)
    a_iota = lax.broadcasted_iota(jnp.int32, (16, CH), 0).astype(F32).astype(BF16)
    zero = BF16(0)
    counts = jnp.zeros((16, 128), F32)
    for k in range(CHUNKS):
        loads[k].wait()
        bh = []
        for g in range(k * (CH // 128), (k + 1) * (CH // 128)):
            upper = jnp.broadcast_to(half_t[:, g : g + 1], (128, 128)) != zero
            v = beh_v[g * 128 : (g + 1) * 128, :].astype(BF16)
            rhs[g * 128 : (g + 1) * 128, :128] = jnp.where(upper, zero, v)
            rhs[g * 128 : (g + 1) * 128, 128:] = jnp.where(upper, v, zero)
            low = jnp.broadcast_to(low_t[:, g : g + 1], (128, 128))
            bh.append(jnp.where(low == lane, BF16(1), zero))
        ab = jnp.broadcast_to(ahot_row[:, k * CH : (k + 1) * CH], (16, CH)).astype(BF16)
        ah = jnp.where(ab == a_iota, BF16(1), zero)
        counts = counts + jnp.dot(ah, jnp.concatenate(bh, axis=0), preferred_element_type=F32)
        for n, part in enumerate(block_sums(0, k * CH, CH)):
            if k == 0:
                acc[n] = part
            else:
                acc[n] += part
    for n in range(2):
        s_send[0, n * 2 * ROWS : (n + 1) * 2 * ROWS, :] = acc[n].astype(BF16)
    cnt_x[...] = counts

    def rs_copy(i, j):
        return remote(
            s_send.at[i, pl.ds(j * ROWS, ROWS), :],
            rs_buf.at[i * 4 + j],
            rs_s.at[0],
            rs_r.at[i],
            (seq_at(*SETS[i][j]), c),
        )

    def cntx_copy(d):
        return remote(cnt_x, cnt_xb.at[d], cnt_s.at[0], cnt_r.at[0], (seq_at(d, 0), c))

    def cnty_copy(d):
        return remote(cnt_y, cnt_yb.at[d], cnt_s.at[1], cnt_r.at[1], (seq_at(0, d), c))

    ops[3].wait()
    pl.semaphore_wait(barrier, 22)
    for d in ORDER:
        cntx_copy(d).start()
    for j in range(4):
        rs_copy(0, j).start()
    for j in range(1, NCAND):
        peer = (c + j) % NCAND
        remote(cand_ref.at[peer], mine.at[c], cand_s.at[0], cand_s.at[1], (s, peer)).start()
    mine[c] = cand_ref[c]

    for i in range(1, 4):
        val = block_sums(i, 0, SLOTS)
        for n in range(2):
            s_send[i, n * 2 * ROWS : (n + 1) * 2 * ROWS, :] = val[n].astype(BF16)
        if i == 3:
            own[...] = val[0][:ROWS]
        for j in range(4):
            if SETS[i][j] != (0, 0):
                rs_copy(i, j).start()

    for cp in ops[4:]:
        cp.wait()
    wait_bytes(mine.at[pl.ds(0, 7)], cand_s.at[1])
    cands = mine[...].reshape(256, 128)
    q = jnp.dot(cands, wq_ref[...], preferred_element_type=F32).astype(BF16)
    q2[...] = nt_dot(q, wk_ref[...]).astype(BF16)
    wt[...] = wh_ref[...].astype(F32).T.astype(BF16)
    bcol[...] = jnp.broadcast_to(bh_ref[...], (128, HID)).T
    wcol[...] = jnp.broadcast_to(wo_ref[...], (128, HID)).T
    hc[...] = nt_dot(wt[:, :D], cands) + jnp.concatenate([bcol[...], bcol[...]], axis=1)
    wait_bytes(cnt_xb.at[pl.ds(1, 3)], cnt_r.at[0])
    cnt_y[...] = cnt_x[...] + cnt_xb[1] + cnt_xb[2] + cnt_xb[3]

    total = own[...]
    for i in range(4):
        slots = range(i * 4 + (i == 3), i * 4 + 4)
        wait_bytes(rs_buf.at[pl.ds(slots[0], len(slots))], rs_r.at[i])
        for k in slots:
            total = total + rs_buf[k].astype(F32)
    tb = total.astype(BF16)

    gs = (ga, gb)

    def at_rows(half, px, py):
        p = py * NX + px if half else px * NY + py
        return gs[half].at[pl.ds(pl.multiple_of(p * ROWS, ROWS), ROWS), :]

    at_rows(0, x, y)[...] = tb[:, :128]
    at_rows(1, x, y)[...] = tb[:, 128:]

    def ag1(half, d):
        blk = at_rows(half, x, y)
        dev = seq_at(0, d) if half else seq_at(d, 0)
        return remote(blk, blk, ag_s.at[half], ag_r.at[half * 6 + d - 1], (dev, c))

    def ag2(half, d, e):
        n = half * 6 + (3, 4, 5, 4)[d]
        if (d, e) == (2, 2):
            blk = at_rows(half, x, y)
            dev = seq_at(2, 2)
        elif half == 0:
            blk = at_rows(0, (x + NX - d) % NX, y)
            dev = seq_at(0, e)
        else:
            blk = at_rows(1, x, (y + NY - d) % NY)
            dev = seq_at(e, 0)
        return remote(blk, blk, ag_s.at[half], ag_r.at[n], (dev, c))

    for d in ORDER:
        for half in range(2):
            ag1(half, d).start()
    for half in range(2):
        ag2(half, 2, 2).start()
    for d in ORDER:
        cnty_copy(d).start()
    for d in (2, 1, 3):
        for half in range(2):
            ag2(half, 0, d).start()
    for d in ORDER:
        for half in range(2):
            ag1(half, d).wait_recv()
            for e in (2, 1, 3):
                if (d, e) != (2, 2):
                    ag2(half, d, e).start()

    wait_bytes(cnt_yb.at[pl.ds(1, 3)], cnt_r.at[1])
    tot = cnt_y[...] + cnt_yb[1] + cnt_yb[2] + cnt_yb[3]
    inv = 1.0 / jnp.maximum(tot, 1.0)
    inv_ref[...] = inv
    mult_ref[...] = inv * (1.0 / jnp.sqrt(F32(D)))
    bias_ref[...] = (
        jnp.where(tot > 0, jnp.log(1.0 + tot), F32(-1e9)).astype(BF16).astype(F32)
    )

    top = den = att = None
    for step, dists in enumerate(((0,), (1, 3), (2,))):
        keys, rows = [], []
        for half in range(2):
            size = 3 * ROWS * len(dists)
            wait_bytes(gs[half].at[pl.ds(0, size), :], ag_r.at[half * 6 + 3 + step])
        for d in dists:
            for half in range(2):
                g = (y + NY - d) % NY if half else (x + NX - d) % NX
                keys.append(gs[half][pl.ds(pl.multiple_of(g * MB, MB), MB), :])
                rows += [half * 8 + g * 2, half * 8 + g * 2 + 1]
        new = None
        for n, kb in enumerate(keys):
            raw = nt_dot(q2[...], kb)
            for j in range(2):
                r = rows[2 * n + j]
                t = raw[:, j * 128 : (j + 1) * 128] * mult_ref[pl.ds(r, 1), :]
                t = t + bias_ref[pl.ds(r, 1), :]
                sc[:, (2 * n + j) * 128 : (2 * n + j + 1) * 128] = t
                new = t if new is None else jnp.maximum(new, t)
        new = jnp.broadcast_to(jnp.max(new, axis=1, keepdims=True), (256, 128))
        if top is not None:
            new = jnp.maximum(top, new)
            alpha = jnp.exp(top - new)
            den = den * alpha
            att = att * alpha
        top = new
        for n, kb in enumerate(keys):
            ps = []
            for j in range(2):
                r = rows[2 * n + j]
                e = jnp.exp(sc[:, (2 * n + j) * 128 : (2 * n + j + 1) * 128] - top)
                den = e if den is None else den + e
                ps.append((e * inv_ref[pl.ds(r, 1), :]).astype(BF16))
            p = jnp.concatenate(ps, axis=1)
            pv = jnp.dot(p, kb, preferred_element_type=F32)
            att = pv if att is None else att + pv
    att = (att / jnp.sum(den, axis=1, keepdims=True)).astype(BF16)

    row = 0.0
    for k in range(2):
        part = slice(k * (HID // 2), (k + 1) * (HID // 2))
        hid = jnp.maximum(hc[part, :] + nt_dot(wt[part, D:], att), 0.0)
        hid = hid * jnp.concatenate([wcol[part, :], wcol[part, :]], axis=1)
        row = row + jnp.sum(hid, axis=0, keepdims=True)
    for j in range(NCAND):
        out_send[j, :, :32] = row[:, j * 32 : (j + 1) * 32]
    for j in range(1, NCAND):
        peer = (c + j) % NCAND
        remote(out_send.at[peer], out_buf.at[c], out_s.at[0], out_s.at[1], (s, peer)).start()
    out_buf[c] = out_send[c]
    wait_bytes(mine.at[pl.ds(0, 7)], cand_s.at[0])
    wait_bytes(cnt_xb.at[pl.ds(1, 3)], cnt_s.at[0])
    wait_bytes(cnt_yb.at[pl.ds(1, 3)], cnt_s.at[1])
    wait_bytes(rs_buf.at[pl.ds(0, 15)], rs_s.at[0])
    for half in range(2):
        wait_bytes(gs[half].at[pl.ds(0, 15 * ROWS), :], ag_s.at[half])
    wait_bytes(out_buf.at[pl.ds(0, 7)], out_s.at[0])
    wait_bytes(out_buf.at[pl.ds(0, 7)], out_s.at[1])
    out_ref[...] = out_buf[:, 0, :32]


def on_device(
    behaviors, cluster_ids, lengths, candidates, w_query, w_key, w_hidden, b_hidden, w_out
):
    vmem = pl.BlockSpec(memory_space=pltpu.VMEM)
    dma = pltpu.SemaphoreType.DMA
    return pl.pallas_call(
        kernel,
        out_shape=pltpu.VMEM((8, 32), F32),
        in_specs=[pl.BlockSpec(memory_space=pltpu.HBM)] * 10,
        out_specs=vmem,
        scratch_shapes=[
            pltpu.SMEM((1, 1), jnp.int32),
            pltpu.VMEM((SLOTS, D), F32),
            pltpu.VMEM((1, SLOTS), jnp.int32),
            pltpu.VMEM((64, 128), jnp.int32),
            pltpu.VMEM((8, 32, D), BF16),
            pltpu.VMEM((D, D), BF16),
            pltpu.VMEM((D, D), BF16),
            pltpu.VMEM((2 * D, HID), BF16),
            pltpu.VMEM((1, HID), F32),
            pltpu.VMEM((1, HID), F32),
            pltpu.VMEM((SLOTS, 2 * D), BF16),
            pltpu.VMEM((16, SLOTS), BF16),
            pltpu.VMEM((16, SLOTS), BF16),
            pltpu.VMEM((2, 2 * ROWS, 2 * D), F32),
            pltpu.VMEM((ROWS, 2 * D), F32),
            pltpu.VMEM((4, MB, 2 * D), BF16),
            pltpu.VMEM((16, ROWS, 2 * D), BF16),
            pltpu.VMEM((16, 128), F32),
            pltpu.VMEM((4, 16, 128), F32),
            pltpu.VMEM((16, 128), F32),
            pltpu.VMEM((4, 16, 128), F32),
            pltpu.VMEM((HALF, D), BF16),
            pltpu.VMEM((HALF, D), BF16),
            pltpu.VMEM((8, 32, D), BF16),
            pltpu.VMEM((256, D), BF16),
            pltpu.VMEM((HID, 2 * D), BF16),
            pltpu.VMEM((HID, 256), F32),
            pltpu.VMEM((HID, 128), F32),
            pltpu.VMEM((HID, 128), F32),
            pltpu.VMEM((8, 1, 128), F32),
            pltpu.VMEM((8, 1, 128), F32),
            pltpu.VMEM((16, 128), F32),
            pltpu.VMEM((16, 128), F32),
            pltpu.VMEM((16, 128), F32),
            pltpu.VMEM((256, 1024), F32),
            dma((CHUNKS,)),
            dma((9,)),
            dma((2,)),
            dma((2,)),
            dma((2,)),
            dma((1,)),
            dma((4,)),
            dma((2,)),
            dma((12,)),
            dma((2,)),
        ],
        compiler_params=pltpu.CompilerParams(collective_id=0, has_side_effects=True),
        name="fused",
    )(
        lengths,
        behaviors,
        cluster_ids,
        cluster_ids.reshape(64, 128),
        candidates,
        w_query,
        w_key,
        w_hidden,
        b_hidden.reshape(1, HID),
        w_out.reshape(1, HID),
    )


def solution(mesh):
    in_specs = (
        P("cand", "seq", None),
        P("cand", "seq"),
        P("cand", "seq"),
        P(None, ("seq", "cand"), None),
        P(),
        P(),
        P(),
        P(),
        P(),
    )
    return jax.shard_map(
        on_device,
        mesh=mesh,
        in_specs=in_specs,
        out_specs=P(None, ("seq", "cand")),
        check_vma=False,
    )
```

```python
import jax
import jax.numpy as jnp
from jax import lax
from jax.experimental import pallas as pl
from jax.experimental.pallas import tpu as pltpu
from jax.sharding import PartitionSpec as P

BF16 = jnp.bfloat16
F32 = jnp.float32
NX, NY, NCAND = 4, 4, 8
SLOTS, D, HID = 8192, 128, 512
HALF = 1024
CHUNKS = 4
CH = SLOTS // CHUNKS
MB = 256
ROWS = HALF // 16


def remote(src, dst, send, recv, device_id):
    return pltpu.make_async_remote_copy(
        src_ref=src,
        dst_ref=dst,
        send_sem=send,
        recv_sem=recv,
        device_id=device_id,
        device_id_type=pl.DeviceIdType.MESH,
    )


def wait_bytes(ref, sem):
    pltpu.make_async_copy(ref, ref, sem).wait()


def nt_dot(a, b):
    return lax.dot_general(a, b, (((1,), (1,)), ((), ())), preferred_element_type=F32)


SETS = (
    ((2, 3), (1, 2), (3, 2), (2, 1)),
    ((1, 1), (1, 3), (3, 1), (3, 3)),
    ((2, 2), (2, 0), (0, 2), (1, 0)),
    ((0, 0), (3, 0), (0, 1), (0, 3)),
)
EARLY = ((2, 3), (2, 1), (2, 2), (2, 0), (0, 2))
LATE = ((0, 1), (0, 3))
ORDER = (1, 3, 2)


def kernel(
    len_hbm,
    beh_hbm,
    ids_hbm,
    ids2_hbm,
    cand_hbm,
    wq_hbm,
    wk_hbm,
    wh_hbm,
    bh_hbm,
    wo_hbm,
    out_ref,
    len_ref,
    beh_v,
    ids_ref,
    ids2_ref,
    cand_ref,
    wq_ref,
    wk_ref,
    wh_ref,
    bh_ref,
    wo_ref,
    rhs,
    own16,
    low16,
    acc,
    own,
    s_send,
    add_buf,
    add_send,
    fin_buf,
    cnt_x,
    cnt_xb,
    cnt_y,
    cnt_yb,
    ga,
    gb,
    mine,
    q2,
    wt,
    hc,
    bcol,
    wcol,
    out_send,
    out_buf,
    inv_ref,
    mult_ref,
    bias_ref,
    sc,
    load_sem,
    op_sem,
    cand_s,
    cnt_s,
    cnt_r,
    rs_s,
    add_r,
    fin_r,
    ag_s,
    ag_r,
    out_s,
):
    s = lax.axis_index("seq")
    c = lax.axis_index("cand")
    x, y = s // NY, s % NY

    pairs = (
        (len_hbm, len_ref),
        (ids_hbm, ids_ref),
        (ids2_hbm, ids2_ref),
        (cand_hbm, cand_ref),
        (wq_hbm, wq_ref),
        (wk_hbm, wk_ref),
        (wh_hbm, wh_ref),
        (bh_hbm, bh_ref),
        (wo_hbm, wo_ref),
    )
    ops = [pltpu.make_async_copy(a, b, op_sem.at[n]) for n, (a, b) in enumerate(pairs)]
    loads = [
        pltpu.make_async_copy(
            beh_hbm.at[0, pl.ds(k * CH, CH), :], beh_v.at[pl.ds(k * CH, CH), :], load_sem.at[k]
        )
        for k in range(CHUNKS)
    ]
    for cp in ops[:3] + loads + ops[3:]:
        cp.start()

    def seq_at(dx, dy):
        return ((x + dx) % NX) * NY + (y + dy) % NY

    barrier = pltpu.get_barrier_semaphore()
    for k in range(1, 16):
        pl.semaphore_signal(
            barrier, inc=1, device_id=(seq_at(k // 4, k % 4), c), device_id_type=pl.DeviceIdType.MESH
        )
    for j in range(1, NCAND):
        pl.semaphore_signal(
            barrier, inc=1, device_id=(s, (c + j) % NCAND), device_id_type=pl.DeviceIdType.MESH
        )

    for cp in ops[:3]:
        cp.wait()
    length = len_ref[0, 0]
    idrow = ids_ref[...]
    live = lax.broadcasted_iota(jnp.int32, (1, SLOTS), 1) < length
    high = (idrow >> 8) & 3
    mid = (idrow >> 6) & 3
    owner_row = jnp.where(idrow >= HALF, mid * 4 + high, high * 4 + mid)
    low_row = jnp.where(live, idrow & (ROWS - 1), 255)
    own16[...] = jnp.broadcast_to(owner_row.astype(F32), (16, SLOTS)).astype(BF16)
    low16[...] = jnp.broadcast_to(low_row.astype(F32), (16, SLOTS)).astype(BF16)
    ahot_row = jnp.where(live, idrow >> 7, 255).astype(F32)
    ids_t = jnp.concatenate([ids2_ref[...], ids2_ref[...]], axis=0).T
    half_t = (ids_t >> 10).astype(F32).astype(BF16)
    low_t = (ids_t & 127).astype(F32).astype(BF16)

    iota16 = lax.broadcasted_iota(jnp.int32, (ROWS, 128), 0).astype(F32).astype(BF16)

    def onehot(owners, k0, kc):
        parts = []
        for dx, dy in owners:
            p16 = jnp.full((16, kc), seq_at(dx, dy).astype(F32), F32).astype(BF16)
            b16 = jnp.where(own16[:, pl.ds(k0, kc)] == p16, low16[:, pl.ds(k0, kc)], BF16(255))
            cols = []
            for t in range(kc // 128):
                bb = jnp.broadcast_to(b16[None, :, t * 128 : (t + 1) * 128], (ROWS // 16, 16, 128))
                cols.append(jnp.where(iota16 == bb.reshape(ROWS, 128), BF16(1), BF16(0)))
            parts.append(jnp.concatenate(cols, axis=1))
        return jnp.concatenate(parts, axis=0)

    def block_sums(i, k0, kc):
        return [
            jnp.dot(onehot(owners, k0, kc), rhs[k0 : k0 + kc, :], preferred_element_type=F32)
            for owners in (SETS[i][:2], SETS[i][2:])
        ]

    lane = lax.broadcasted_iota(jnp.int32, (128, 128), 1).astype(F32).astype(BF16)
    a_iota = lax.broadcasted_iota(jnp.int32, (16, CH), 0).astype(F32).astype(BF16)
    zero = BF16(0)
    counts = jnp.zeros((16, 128), F32)
    for k in range(CHUNKS):
        loads[k].wait()
        bh = []
        for g in range(k * (CH // 128), (k + 1) * (CH // 128)):
            upper = jnp.broadcast_to(half_t[:, g : g + 1], (128, 128)) != zero
            v = beh_v[g * 128 : (g + 1) * 128, :].astype(BF16)
            rhs[g * 128 : (g + 1) * 128, :128] = jnp.where(upper, zero, v)
            rhs[g * 128 : (g + 1) * 128, 128:] = jnp.where(upper, v, zero)
            low = jnp.broadcast_to(low_t[:, g : g + 1], (128, 128))
            bh.append(jnp.where(low == lane, BF16(1), zero))
        ab = jnp.broadcast_to(ahot_row[:, k * CH : (k + 1) * CH], (16, CH)).astype(BF16)
        ah = jnp.where(ab == a_iota, BF16(1), zero)
        counts = counts + jnp.dot(ah, jnp.concatenate(bh, axis=0), preferred_element_type=F32)
        for n, part in enumerate(block_sums(0, k * CH, CH)):
            if k == 0:
                acc[n] = part
            else:
                acc[n] += part
    for n in range(2):
        s_send[0, n * 2 * ROWS : (n + 1) * 2 * ROWS, :] = acc[n].astype(BF16)
    cnt_x[...] = counts

    def flip(half, p, q):
        return (q, p) if half else (p, q)

    def rs_start(i):
        for j, offset in enumerate(SETS[i]):
            for half in range(2):
                p, q = flip(half, *offset)
                src = s_send.at[i, pl.ds(j * ROWS, ROWS), pl.ds(half * D, D)]
                if p % 2 and q:
                    remote(
                        src,
                        add_buf.at[half, p // 2 * 3 + q - 1],
                        rs_s.at[0],
                        add_r.at[half],
                        (seq_at(*flip(half, 0, q)), c),
                    ).start()
                elif (p, q) in EARLY:
                    dst = fin_buf.at[half, EARLY.index((p, q))]
                    remote(
                        src, dst, rs_s.at[1], fin_r.at[half], (seq_at(*offset), c)
                    ).start()
                elif (p, q) in LATE:
                    dst = fin_buf.at[half, 5 + LATE.index((p, q))]
                    remote(
                        src, dst, rs_s.at[1], fin_r.at[2 + half], (seq_at(*offset), c)
                    ).start()

    def add_and_send():
        for half in range(2):
            wait_bytes(add_buf.at[half], add_r.at[half])
            for n, p in enumerate((1, 3)):
                offset = flip(half, p, 0)
                i, j = next((i, z.index(offset)) for i, z in enumerate(SETS) if offset in z)
                val = s_send[i, j * ROWS : (j + 1) * ROWS, half * D : (half + 1) * D].astype(F32)
                for q in range(3):
                    val = val + add_buf[half, n * 3 + q].astype(F32)
                add_send[half, n] = val.astype(BF16)
        for half in range(2):
            for n, p in enumerate((1, 3)):
                remote(
                    add_send.at[half, n],
                    fin_buf.at[half, 7 + n],
                    rs_s.at[1],
                    fin_r.at[2 + half],
                    (seq_at(*flip(half, p, 0)), c),
                ).start()

    def cntx_copy(d):
        return remote(cnt_x, cnt_xb.at[d], cnt_s.at[0], cnt_r.at[0], (seq_at(d, 0), c))

    def cnty_copy(d):
        return remote(cnt_y, cnt_yb.at[d], cnt_s.at[1], cnt_r.at[1], (seq_at(0, d), c))

    ops[3].wait()
    pl.semaphore_wait(barrier, 22)
    for d in ORDER:
        cntx_copy(d).start()
    rs_start(0)
    for j in range(1, NCAND):
        peer = (c + j) % NCAND
        remote(cand_ref.at[peer], mine.at[c], cand_s.at[0], cand_s.at[1], (s, peer)).start()
    mine[c] = cand_ref[c]

    for i in range(1, 4):
        val = block_sums(i, 0, SLOTS)
        for n in range(2):
            s_send[i, n * 2 * ROWS : (n + 1) * 2 * ROWS, :] = val[n].astype(BF16)
        if i == 3:
            own[...] = val[0][:ROWS]
        rs_start(i)
    add_and_send()

    for cp in ops[4:]:
        cp.wait()
    wait_bytes(mine.at[pl.ds(0, 7)], cand_s.at[1])
    cands = mine[...].reshape(256, 128)
    q = jnp.dot(cands, wq_ref[...], preferred_element_type=F32).astype(BF16)
    q2[...] = nt_dot(q, wk_ref[...]).astype(BF16)
    wt[...] = wh_ref[...].astype(F32).T.astype(BF16)
    bcol[...] = jnp.broadcast_to(bh_ref[...], (128, HID)).T
    wcol[...] = jnp.broadcast_to(wo_ref[...], (128, HID)).T
    hc[...] = nt_dot(wt[:, :D], cands) + jnp.concatenate([bcol[...], bcol[...]], axis=1)
    wait_bytes(cnt_xb.at[pl.ds(1, 3)], cnt_r.at[0])
    cnt_y[...] = cnt_x[...] + cnt_xb[1] + cnt_xb[2] + cnt_xb[3]

    halves = []
    for half in range(2):
        total = own[:, half * D : (half + 1) * D]
        wait_bytes(fin_buf.at[half, pl.ds(0, 5)], fin_r.at[half])
        for k in range(5):
            total = total + fin_buf[half, k].astype(F32)
        halves.append(total)
    for half in range(2):
        wait_bytes(fin_buf.at[half, pl.ds(5, 4)], fin_r.at[2 + half])
        for k in range(5, 9):
            halves[half] = halves[half] + fin_buf[half, k].astype(F32)

    gs = (ga, gb)

    def at_rows(half, px, py):
        p = py * NX + px if half else px * NY + py
        return gs[half].at[pl.ds(pl.multiple_of(p * ROWS, ROWS), ROWS), :]

    for half in range(2):
        at_rows(half, x, y)[...] = halves[half].astype(BF16)

    def ag_copy(half, via, p, q):
        blk = at_rows(half, *[(z + 4 - w) % 4 for z, w in zip((x, y), flip(half, via, 0))])
        n = half * 5 + (0 if p == 0 else 1 if p == 2 else 2 if q else 3 + p // 2)
        dev = seq_at(*flip(half, p - via, q))
        return remote(blk, blk, ag_s.at[half], ag_r.at[n], (dev, c))

    for p in ORDER:
        for half in range(2):
            ag_copy(half, 0, p, 0).start()
    for p, q in ((2, 2), (1, 2), (3, 2), (2, 1), (2, 3), (0, 2), (0, 1), (0, 3)):
        for half in range(2):
            ag_copy(half, 0, p, q).start()
    for d in ORDER:
        cnty_copy(d).start()
    for p in (1, 3):
        for half in range(2):
            ag_copy(half, 0, p, 0).wait_recv()
            for q in (1, 3):
                ag_copy(half, p, p, q).start()
    wait_bytes(cnt_yb.at[pl.ds(1, 3)], cnt_r.at[1])
    tot = cnt_y[...] + cnt_yb[1] + cnt_yb[2] + cnt_yb[3]
    inv = 1.0 / jnp.maximum(tot, 1.0)
    inv_ref[...] = inv
    mult_ref[...] = inv * (1.0 / jnp.sqrt(F32(D)))
    bias_ref[...] = (
        jnp.where(tot > 0, jnp.log(1.0 + tot), F32(-1e9)).astype(BF16).astype(F32)
    )

    top = den = att = None
    for step, dists in enumerate(((0,), (2,), (1, 3))):
        keys, rows = [], []
        for half in range(2):
            size = (3, 4, 6)[step] * ROWS
            wait_bytes(gs[half].at[pl.ds(0, size), :], ag_r.at[half * 5 + step])
        for d in dists:
            for half in range(2):
                g = (y + NY - d) % NY if half else (x + NX - d) % NX
                keys.append(gs[half][pl.ds(pl.multiple_of(g * MB, MB), MB), :])
                rows += [half * 8 + g * 2, half * 8 + g * 2 + 1]
        new = None
        for n, kb in enumerate(keys):
            raw = nt_dot(q2[...], kb)
            for j in range(2):
                r = rows[2 * n + j]
                t = raw[:, j * 128 : (j + 1) * 128] * mult_ref[pl.ds(r, 1), :]
                t = t + bias_ref[pl.ds(r, 1), :]
                sc[:, (2 * n + j) * 128 : (2 * n + j + 1) * 128] = t
                new = t if new is None else jnp.maximum(new, t)
        new = jnp.broadcast_to(jnp.max(new, axis=1, keepdims=True), (256, 128))
        if top is not None:
            new = jnp.maximum(top, new)
            alpha = jnp.exp(top - new)
            den = den * alpha
            att = att * alpha
        top = new
        for n, kb in enumerate(keys):
            ps = []
            for j in range(2):
                r = rows[2 * n + j]
                e = jnp.exp(sc[:, (2 * n + j) * 128 : (2 * n + j + 1) * 128] - top)
                den = e if den is None else den + e
                ps.append((e * inv_ref[pl.ds(r, 1), :]).astype(BF16))
            p = jnp.concatenate(ps, axis=1)
            pv = jnp.dot(p, kb, preferred_element_type=F32)
            att = pv if att is None else att + pv
    att = (att / jnp.sum(den, axis=1, keepdims=True)).astype(BF16)

    row = 0.0
    for k in range(2):
        part = slice(k * (HID // 2), (k + 1) * (HID // 2))
        hid = jnp.maximum(hc[part, :] + nt_dot(wt[part, D:], att), 0.0)
        hid = hid * jnp.concatenate([wcol[part, :], wcol[part, :]], axis=1)
        row = row + jnp.sum(hid, axis=0, keepdims=True)
    for j in range(NCAND):
        out_send[j, :, :32] = row[:, j * 32 : (j + 1) * 32]
    for j in range(1, NCAND):
        peer = (c + j) % NCAND
        remote(out_send.at[peer], out_buf.at[c], out_s.at[0], out_s.at[1], (s, peer)).start()
    out_buf[c] = out_send[c]
    wait_bytes(mine.at[pl.ds(0, 7)], cand_s.at[0])
    wait_bytes(cnt_xb.at[pl.ds(1, 3)], cnt_s.at[0])
    wait_bytes(cnt_yb.at[pl.ds(1, 3)], cnt_s.at[1])
    wait_bytes(add_buf, rs_s.at[0])
    wait_bytes(fin_buf, rs_s.at[1])
    for half in range(2):
        wait_bytes(gs[half].at[pl.ds(0, 15 * ROWS), :], ag_s.at[half])
    wait_bytes(out_buf.at[pl.ds(0, 7)], out_s.at[0])
    wait_bytes(out_buf.at[pl.ds(0, 7)], out_s.at[1])
    out_ref[...] = out_buf[:, 0, :32]


def on_device(
    behaviors, cluster_ids, lengths, candidates, w_query, w_key, w_hidden, b_hidden, w_out
):
    vmem = pl.BlockSpec(memory_space=pltpu.VMEM)
    dma = pltpu.SemaphoreType.DMA
    return pl.pallas_call(
        kernel,
        out_shape=pltpu.VMEM((8, 32), F32),
        in_specs=[pl.BlockSpec(memory_space=pltpu.HBM)] * 10,
        out_specs=vmem,
        scratch_shapes=[
            pltpu.SMEM((1, 1), jnp.int32),
            pltpu.VMEM((SLOTS, D), F32),
            pltpu.VMEM((1, SLOTS), jnp.int32),
            pltpu.VMEM((64, 128), jnp.int32),
            pltpu.VMEM((8, 32, D), BF16),
            pltpu.VMEM((D, D), BF16),
            pltpu.VMEM((D, D), BF16),
            pltpu.VMEM((2 * D, HID), BF16),
            pltpu.VMEM((1, HID), F32),
            pltpu.VMEM((1, HID), F32),
            pltpu.VMEM((SLOTS, 2 * D), BF16),
            pltpu.VMEM((16, SLOTS), BF16),
            pltpu.VMEM((16, SLOTS), BF16),
            pltpu.VMEM((2, 2 * ROWS, 2 * D), F32),
            pltpu.VMEM((ROWS, 2 * D), F32),
            pltpu.VMEM((4, MB, 2 * D), BF16),
            pltpu.VMEM((2, 6, ROWS, D), BF16),
            pltpu.VMEM((2, 2, ROWS, D), BF16),
            pltpu.VMEM((2, 9, ROWS, D), BF16),
            pltpu.VMEM((16, 128), F32),
            pltpu.VMEM((4, 16, 128), F32),
            pltpu.VMEM((16, 128), F32),
            pltpu.VMEM((4, 16, 128), F32),
            pltpu.VMEM((HALF, D), BF16),
            pltpu.VMEM((HALF, D), BF16),
            pltpu.VMEM((8, 32, D), BF16),
            pltpu.VMEM((256, D), BF16),
            pltpu.VMEM((HID, 2 * D), BF16),
            pltpu.VMEM((HID, 256), F32),
            pltpu.VMEM((HID, 128), F32),
            pltpu.VMEM((HID, 128), F32),
            pltpu.VMEM((8, 1, 128), F32),
            pltpu.VMEM((8, 1, 128), F32),
            pltpu.VMEM((16, 128), F32),
            pltpu.VMEM((16, 128), F32),
            pltpu.VMEM((16, 128), F32),
            pltpu.VMEM((256, 1024), F32),
            dma((CHUNKS,)),
            dma((9,)),
            dma((2,)),
            dma((2,)),
            dma((2,)),
            dma((2,)),
            dma((2,)),
            dma((4,)),
            dma((2,)),
            dma((10,)),
            dma((2,)),
        ],
        compiler_params=pltpu.CompilerParams(collective_id=0, has_side_effects=True),
        name="fused",
    )(
        lengths,
        behaviors,
        cluster_ids,
        cluster_ids.reshape(64, 128),
        candidates,
        w_query,
        w_key,
        w_hidden,
        b_hidden.reshape(1, HID),
        w_out.reshape(1, HID),
    )


def solution(mesh):
    in_specs = (
        P("cand", "seq", None),
        P("cand", "seq"),
        P("cand", "seq"),
        P(None, ("seq", "cand"), None),
        P(),
        P(),
        P(),
        P(),
        P(),
    )
    return jax.shard_map(
        on_device,
        mesh=mesh,
        in_specs=in_specs,
        out_specs=P(None, ("seq", "cand")),
        check_vma=False,
    )
```

```python
import jax
import jax.numpy as jnp
from jax import lax
from jax.experimental import pallas as pl
from jax.experimental.pallas import tpu as pltpu
from jax.sharding import PartitionSpec as P

BF16 = jnp.bfloat16
F32 = jnp.float32
NX, NY, NCAND = 4, 4, 8
SLOTS, D, HID = 8192, 128, 512
HALF = 1024
CHUNKS = 4
CH = SLOTS // CHUNKS
MB = 256
ROWS = HALF // 16


def remote(src, dst, send, recv, device_id):
    return pltpu.make_async_remote_copy(
        src_ref=src,
        dst_ref=dst,
        send_sem=send,
        recv_sem=recv,
        device_id=device_id,
        device_id_type=pl.DeviceIdType.MESH,
    )


def wait_bytes(ref, sem):
    pltpu.make_async_copy(ref, ref, sem).wait()


def nt_dot(a, b):
    return lax.dot_general(a, b, (((1,), (1,)), ((), ())), preferred_element_type=F32)


SETS = (
    ((2, 2), (2, 1), (2, 3), (1, 2)),
    ((3, 2), (1, 1), (1, 3), (3, 1)),
    ((3, 3), (2, 0), (0, 2), (1, 0)),
    ((0, 0), (3, 0), (0, 1), (0, 3)),
)
ORDER = (1, 3, 2)


def kernel(
    len_hbm,
    beh_hbm,
    ids_hbm,
    ids2_hbm,
    cand_hbm,
    wq_hbm,
    wk_hbm,
    wh_hbm,
    bh_hbm,
    wo_hbm,
    out_ref,
    len_ref,
    beh_v,
    ids_ref,
    ids2_ref,
    cand_ref,
    wq_ref,
    wk_ref,
    wh_ref,
    bh_ref,
    wo_ref,
    rhs,
    own16,
    low16,
    acc,
    own,
    s_send,
    add_buf,
    add_send,
    fin_buf,
    cnt_x,
    cnt_xb,
    cnt_y,
    cnt_yb,
    ga,
    gb,
    mine,
    q2,
    wt,
    hc,
    bcol,
    wcol,
    out_send,
    out_buf,
    inv_ref,
    mult_ref,
    bias_ref,
    sc,
    load_sem,
    op_sem,
    cand_s,
    cnt_s,
    cnt_r,
    rs_s,
    add_r,
    fin_r,
    ag_s,
    ag_r,
    out_s,
):
    s = lax.axis_index("seq")
    c = lax.axis_index("cand")
    x, y = s // NY, s % NY

    pairs = (
        (len_hbm, len_ref),
        (ids_hbm, ids_ref),
        (ids2_hbm, ids2_ref),
        (cand_hbm, cand_ref),
        (wq_hbm, wq_ref),
        (wk_hbm, wk_ref),
        (wh_hbm, wh_ref),
        (bh_hbm, bh_ref),
        (wo_hbm, wo_ref),
    )
    ops = [pltpu.make_async_copy(a, b, op_sem.at[n]) for n, (a, b) in enumerate(pairs)]
    loads = [
        pltpu.make_async_copy(
            beh_hbm.at[0, pl.ds(k * CH, CH), :], beh_v.at[pl.ds(k * CH, CH), :], load_sem.at[k]
        )
        for k in range(CHUNKS)
    ]
    for cp in ops[:3] + loads + ops[3:]:
        cp.start()

    def seq_at(dx, dy):
        return ((x + dx) % NX) * NY + (y + dy) % NY

    barrier = pltpu.get_barrier_semaphore()
    for k in range(1, 16):
        pl.semaphore_signal(
            barrier, inc=1, device_id=(seq_at(k // 4, k % 4), c), device_id_type=pl.DeviceIdType.MESH
        )
    for j in range(1, NCAND):
        pl.semaphore_signal(
            barrier, inc=1, device_id=(s, (c + j) % NCAND), device_id_type=pl.DeviceIdType.MESH
        )

    for cp in ops[:3]:
        cp.wait()
    length = len_ref[0, 0]
    idrow = ids_ref[...]
    live = lax.broadcasted_iota(jnp.int32, (1, SLOTS), 1) < length
    high = (idrow >> 8) & 3
    mid = (idrow >> 6) & 3
    owner_row = jnp.where(idrow >= HALF, mid * 4 + high, high * 4 + mid)
    low_row = jnp.where(live, idrow & (ROWS - 1), 255)
    own16[...] = jnp.broadcast_to(owner_row.astype(F32), (16, SLOTS)).astype(BF16)
    low16[...] = jnp.broadcast_to(low_row.astype(F32), (16, SLOTS)).astype(BF16)
    ahot_row = jnp.where(live, idrow >> 7, 255).astype(F32)
    ids_t = jnp.concatenate([ids2_ref[...], ids2_ref[...]], axis=0).T
    half_t = (ids_t >> 10).astype(F32).astype(BF16)
    low_t = (ids_t & 127).astype(F32).astype(BF16)

    iota16 = lax.broadcasted_iota(jnp.int32, (ROWS, 128), 0).astype(F32).astype(BF16)

    def onehot(owners, k0, kc):
        parts = []
        for dx, dy in owners:
            p16 = jnp.full((16, kc), seq_at(dx, dy).astype(F32), F32).astype(BF16)
            b16 = jnp.where(own16[:, pl.ds(k0, kc)] == p16, low16[:, pl.ds(k0, kc)], BF16(255))
            cols = []
            for t in range(kc // 128):
                bb = jnp.broadcast_to(b16[None, :, t * 128 : (t + 1) * 128], (ROWS // 16, 16, 128))
                cols.append(jnp.where(iota16 == bb.reshape(ROWS, 128), BF16(1), BF16(0)))
            parts.append(jnp.concatenate(cols, axis=1))
        return jnp.concatenate(parts, axis=0)

    def block_sums(i, k0, kc):
        rows = jnp.concatenate([rhs[0, k0 : k0 + kc, :], rhs[1, k0 : k0 + kc, :]], axis=1)
        return [
            jnp.dot(onehot(owners, k0, kc), rows, preferred_element_type=F32)
            for owners in (SETS[i][:2], SETS[i][2:])
        ]

    def put_sums(i, n, val):
        for half in range(2):
            s_send[half, i, n * 2 * ROWS : (n + 1) * 2 * ROWS, :] = val[
                :, half * D : (half + 1) * D
            ].astype(BF16)

    lane = lax.broadcasted_iota(jnp.int32, (128, 128), 1).astype(F32).astype(BF16)
    a_iota = lax.broadcasted_iota(jnp.int32, (16, CH), 0).astype(F32).astype(BF16)
    zero = BF16(0)
    counts = jnp.zeros((16, 128), F32)
    for k in range(CHUNKS):
        loads[k].wait()
        bh = []
        for g in range(k * (CH // 128), (k + 1) * (CH // 128)):
            upper = jnp.broadcast_to(half_t[:, g : g + 1], (128, 128)) != zero
            v = beh_v[g * 128 : (g + 1) * 128, :].astype(BF16)
            rhs[0, g * 128 : (g + 1) * 128, :] = jnp.where(upper, zero, v)
            rhs[1, g * 128 : (g + 1) * 128, :] = jnp.where(upper, v, zero)
            low = jnp.broadcast_to(low_t[:, g : g + 1], (128, 128))
            bh.append(jnp.where(low == lane, BF16(1), zero))
        ab = jnp.broadcast_to(ahot_row[:, k * CH : (k + 1) * CH], (16, CH)).astype(BF16)
        ah = jnp.where(ab == a_iota, BF16(1), zero)
        counts = counts + jnp.dot(ah, jnp.concatenate(bh, axis=0), preferred_element_type=F32)
        for n, part in enumerate(block_sums(0, k * CH, CH)):
            if k == 0:
                acc[n] = part
            else:
                acc[n] += part
    for n in range(2):
        put_sums(0, n, acc[n])
    cnt_x[...] = counts

    def flip(half, p, q):
        return (q, p) if half else (p, q)

    def rs_start(i):
        for j, offset in enumerate(SETS[i]):
            for half in range(2):
                p, q = flip(half, *offset)
                src = s_send.at[half, i, pl.ds(j * ROWS, ROWS), :]
                if p and q:
                    remote(
                        src,
                        add_buf.at[half, p - 1, q - 1],
                        rs_s.at[0],
                        add_r.at[half * 3 + p - 1],
                        (seq_at(*flip(half, 0, q)), c),
                    ).start()
                elif q:
                    dst = fin_buf.at[half, q - 1]
                    remote(
                        src, dst, rs_s.at[1], fin_r.at[half], (seq_at(*offset), c)
                    ).start()

    def add_and_send():
        for p in (2, 1, 3):
            for half in range(2):
                wait_bytes(add_buf.at[half, p - 1], add_r.at[half * 3 + p - 1])
                offset = flip(half, p, 0)
                i, j = next((i, z.index(offset)) for i, z in enumerate(SETS) if offset in z)
                val = s_send[half, i, j * ROWS : (j + 1) * ROWS, :].astype(F32)
                for q in range(3):
                    val = val + add_buf[half, p - 1, q].astype(F32)
                add_send[half, p - 1] = val.astype(BF16)
            for half in range(2):
                remote(
                    add_send.at[half, p - 1],
                    fin_buf.at[half, 2 + p],
                    rs_s.at[1],
                    fin_r.at[half],
                    (seq_at(*flip(half, p, 0)), c),
                ).start()

    def cntx_copy(d):
        return remote(cnt_x, cnt_xb.at[d], cnt_s.at[0], cnt_r.at[0], (seq_at(d, 0), c))

    def cnty_copy(d):
        return remote(cnt_y, cnt_yb.at[d], cnt_s.at[1], cnt_r.at[1], (seq_at(0, d), c))

    ops[3].wait()
    pl.semaphore_wait(barrier, 22)
    for d in ORDER:
        cntx_copy(d).start()
    rs_start(0)
    for j in range(1, NCAND):
        peer = (c + j) % NCAND
        remote(cand_ref.at[peer], mine.at[c], cand_s.at[0], cand_s.at[1], (s, peer)).start()
    mine[c] = cand_ref[c]

    for i in range(1, 4):
        val = block_sums(i, 0, SLOTS)
        for n in range(2):
            put_sums(i, n, val[n])
        if i == 3:
            own[...] = val[0][:ROWS]
        rs_start(i)
    add_and_send()

    for cp in ops[4:]:
        cp.wait()
    wait_bytes(mine.at[pl.ds(0, 7)], cand_s.at[1])
    cands = mine[...].reshape(256, 128)
    q = jnp.dot(cands, wq_ref[...], preferred_element_type=F32).astype(BF16)
    q2[...] = nt_dot(q, wk_ref[...]).astype(BF16)
    wt[...] = wh_ref[...].astype(F32).T.astype(BF16)
    bcol[...] = jnp.broadcast_to(bh_ref[...], (128, HID)).T
    wcol[...] = jnp.broadcast_to(wo_ref[...], (128, HID)).T
    hc[...] = nt_dot(wt[:, :D], cands) + jnp.concatenate([bcol[...], bcol[...]], axis=1)
    wait_bytes(cnt_xb.at[pl.ds(1, 3)], cnt_r.at[0])
    cnt_y[...] = cnt_x[...] + cnt_xb[1] + cnt_xb[2] + cnt_xb[3]

    halves = []
    for half in range(2):
        total = own[:, half * D : (half + 1) * D]
        wait_bytes(fin_buf.at[half], fin_r.at[half])
        for k in range(6):
            total = total + fin_buf[half, k].astype(F32)
        halves.append(total)

    gs = (ga, gb)

    def at_rows(half, px, py):
        p = py * NX + px if half else px * NY + py
        return gs[half].at[pl.ds(pl.multiple_of(p * ROWS, ROWS), ROWS), :]

    for half in range(2):
        at_rows(half, x, y)[...] = halves[half].astype(BF16)

    def ag_copy(half, via, p, q):
        blk = at_rows(half, *[(z + 4 - w) % 4 for z, w in zip((x, y), flip(half, via, 0))])
        n = half * 6 + ((0, 1, 2, 1)[p] if p == 0 or q else 2 + p)
        dev = seq_at(*flip(half, p - via, q))
        return remote(blk, blk, ag_s.at[half], ag_r.at[n], (dev, c))

    for p in ORDER:
        for half in range(2):
            ag_copy(half, 0, p, 0).start()
    first = c % 2 == 0

    def far(relayed):
        for p, q in ((1, 2), (3, 2), (2, 1), (2, 3)):
            for half in range(2):
                if not relayed:
                    ag_copy(half, 0, p, q).start()
                elif relayed == p:
                    ag_copy(half, p, p, q).start()

    for half in range(2):
        ag_copy(half, 0, 2, 2).start()
    pl.when(first)(lambda: far(0))
    for q in (2, 1, 3):
        for half in range(2):
            ag_copy(half, 0, 0, q).start()
    for d in ORDER:
        cnty_copy(d).start()
    for p in (1, 3):
        for half in range(2):
            ag_copy(half, 0, p, 0).wait_recv()
            for q in (1, 3):
                ag_copy(half, p, p, q).start()
        pl.when(jnp.logical_not(first))(lambda p=p: far(p))
    for half in range(2):
        ag_copy(half, 0, 2, 0).wait_recv()
    pl.when(jnp.logical_not(first))(lambda: far(2))
    wait_bytes(cnt_yb.at[pl.ds(1, 3)], cnt_r.at[1])
    tot = cnt_y[...] + cnt_yb[1] + cnt_yb[2] + cnt_yb[3]
    inv = 1.0 / jnp.maximum(tot, 1.0)
    inv_ref[...] = inv
    mult_ref[...] = inv * (1.0 / jnp.sqrt(F32(D)))
    bias_ref[...] = (
        jnp.where(tot > 0, jnp.log(1.0 + tot), F32(-1e9)).astype(BF16).astype(F32)
    )

    top = den = att = None
    for step, dists in ((0, (0,)), (2, (2,)), (1, (1, 3))):
        keys, rows = [], []
        for half in range(2):
            size = (3, 6, 3)[step] * ROWS
            wait_bytes(gs[half].at[pl.ds(0, size), :], ag_r.at[half * 6 + step])
        for d in dists:
            for half in range(2):
                g = (y + NY - d) % NY if half else (x + NX - d) % NX
                keys.append(gs[half][pl.ds(pl.multiple_of(g * MB, MB), MB), :])
                rows += [half * 8 + g * 2, half * 8 + g * 2 + 1]
        new = None
        for n, kb in enumerate(keys):
            raw = nt_dot(q2[...], kb)
            for j in range(2):
                r = rows[2 * n + j]
                t = raw[:, j * 128 : (j + 1) * 128] * mult_ref[pl.ds(r, 1), :]
                t = t + bias_ref[pl.ds(r, 1), :]
                sc[:, (2 * n + j) * 128 : (2 * n + j + 1) * 128] = t
                new = t if new is None else jnp.maximum(new, t)
        new = jnp.broadcast_to(jnp.max(new, axis=1, keepdims=True), (256, 128))
        if top is not None:
            new = jnp.maximum(top, new)
            alpha = jnp.exp(top - new)
            den = den * alpha
            att = att * alpha
        top = new
        for n, kb in enumerate(keys):
            ps = []
            for j in range(2):
                r = rows[2 * n + j]
                e = jnp.exp(sc[:, (2 * n + j) * 128 : (2 * n + j + 1) * 128] - top)
                den = e if den is None else den + e
                ps.append((e * inv_ref[pl.ds(r, 1), :]).astype(BF16))
            p = jnp.concatenate(ps, axis=1)
            pv = jnp.dot(p, kb, preferred_element_type=F32)
            att = pv if att is None else att + pv
    att = (att / jnp.sum(den, axis=1, keepdims=True)).astype(BF16)

    row = 0.0
    for k in range(2):
        part = slice(k * (HID // 2), (k + 1) * (HID // 2))
        hid = jnp.maximum(hc[part, :] + nt_dot(wt[part, D:], att), 0.0)
        hid = hid * jnp.concatenate([wcol[part, :], wcol[part, :]], axis=1)
        row = row + jnp.sum(hid, axis=0, keepdims=True)
    for j in range(NCAND):
        out_send[j, :, :32] = row[:, j * 32 : (j + 1) * 32]
    for j in range(1, NCAND):
        peer = (c + j) % NCAND
        remote(out_send.at[peer], out_buf.at[c], out_s.at[0], out_s.at[1], (s, peer)).start()
    out_buf[c] = out_send[c]
    wait_bytes(mine.at[pl.ds(0, 7)], cand_s.at[0])
    wait_bytes(cnt_xb.at[pl.ds(1, 3)], cnt_s.at[0])
    wait_bytes(cnt_yb.at[pl.ds(1, 3)], cnt_s.at[1])
    wait_bytes(add_buf, rs_s.at[0])
    wait_bytes(fin_buf, rs_s.at[1])
    for half in range(2):
        wait_bytes(gs[half].at[pl.ds(0, 15 * ROWS), :], ag_s.at[half])
    wait_bytes(out_buf.at[pl.ds(0, 7)], out_s.at[0])
    wait_bytes(out_buf.at[pl.ds(0, 7)], out_s.at[1])
    out_ref[...] = out_buf[:, 0, :32]


def on_device(
    behaviors, cluster_ids, lengths, candidates, w_query, w_key, w_hidden, b_hidden, w_out
):
    vmem = pl.BlockSpec(memory_space=pltpu.VMEM)
    dma = pltpu.SemaphoreType.DMA
    return pl.pallas_call(
        kernel,
        out_shape=pltpu.VMEM((8, 32), F32),
        in_specs=[pl.BlockSpec(memory_space=pltpu.HBM)] * 10,
        out_specs=vmem,
        scratch_shapes=[
            pltpu.SMEM((1, 1), jnp.int32),
            pltpu.VMEM((SLOTS, D), F32),
            pltpu.VMEM((1, SLOTS), jnp.int32),
            pltpu.VMEM((64, 128), jnp.int32),
            pltpu.VMEM((8, 32, D), BF16),
            pltpu.VMEM((D, D), BF16),
            pltpu.VMEM((D, D), BF16),
            pltpu.VMEM((2 * D, HID), BF16),
            pltpu.VMEM((1, HID), F32),
            pltpu.VMEM((1, HID), F32),
            pltpu.VMEM((2, SLOTS, D), BF16),
            pltpu.VMEM((16, SLOTS), BF16),
            pltpu.VMEM((16, SLOTS), BF16),
            pltpu.VMEM((2, 2 * ROWS, 2 * D), F32),
            pltpu.VMEM((ROWS, 2 * D), F32),
            pltpu.VMEM((2, 4, MB, D), BF16),
            pltpu.VMEM((2, 3, 3, ROWS, D), BF16),
            pltpu.VMEM((2, 3, ROWS, D), BF16),
            pltpu.VMEM((2, 6, ROWS, D), BF16),
            pltpu.VMEM((16, 128), F32),
            pltpu.VMEM((4, 16, 128), F32),
            pltpu.VMEM((16, 128), F32),
            pltpu.VMEM((4, 16, 128), F32),
            pltpu.VMEM((HALF, D), BF16),
            pltpu.VMEM((HALF, D), BF16),
            pltpu.VMEM((8, 32, D), BF16),
            pltpu.VMEM((256, D), BF16),
            pltpu.VMEM((HID, 2 * D), BF16),
            pltpu.VMEM((HID, 256), F32),
            pltpu.VMEM((HID, 128), F32),
            pltpu.VMEM((HID, 128), F32),
            pltpu.VMEM((8, 1, 128), F32),
            pltpu.VMEM((8, 1, 128), F32),
            pltpu.VMEM((16, 128), F32),
            pltpu.VMEM((16, 128), F32),
            pltpu.VMEM((16, 128), F32),
            pltpu.VMEM((256, 1024), F32),
            dma((CHUNKS,)),
            dma((9,)),
            dma((2,)),
            dma((2,)),
            dma((2,)),
            dma((2,)),
            dma((6,)),
            dma((2,)),
            dma((2,)),
            dma((12,)),
            dma((2,)),
        ],
        compiler_params=pltpu.CompilerParams(collective_id=0, has_side_effects=True),
        name="fused",
    )(
        lengths,
        behaviors,
        cluster_ids,
        cluster_ids.reshape(64, 128),
        candidates,
        w_query,
        w_key,
        w_hidden,
        b_hidden.reshape(1, HID),
        w_out.reshape(1, HID),
    )


def solution(mesh):
    in_specs = (
        P("cand", "seq", None),
        P("cand", "seq"),
        P("cand", "seq"),
        P(None, ("seq", "cand"), None),
        P(),
        P(),
        P(),
        P(),
        P(),
    )
    return jax.shard_map(
        on_device,
        mesh=mesh,
        in_specs=in_specs,
        out_specs=P(None, ("seq", "cand")),
        check_vma=False,
    )
```

```python
import jax
import jax.numpy as jnp
from jax import lax
from jax.experimental import pallas as pl
from jax.experimental.pallas import tpu as pltpu
from jax.sharding import PartitionSpec as P

BF16 = jnp.bfloat16
F32 = jnp.float32
NX, NY, NCAND = 4, 4, 8
SLOTS, D, HID = 8192, 128, 512
HALF = 1024
CHUNKS = 4
CH = SLOTS // CHUNKS
MB = 256
ROWS = HALF // 16


def remote(src, dst, send, recv, device_id):
    return pltpu.make_async_remote_copy(
        src_ref=src,
        dst_ref=dst,
        send_sem=send,
        recv_sem=recv,
        device_id=device_id,
        device_id_type=pl.DeviceIdType.MESH,
    )


def wait_bytes(ref, sem):
    pltpu.make_async_copy(ref, ref, sem).wait()


def nt_dot(a, b):
    return lax.dot_general(a, b, (((1,), (1,)), ((), ())), preferred_element_type=F32)


SETS = (
    ((2, 2), (2, 1), (2, 3), (1, 2)),
    ((3, 2), (1, 1), (1, 3), (3, 1)),
    ((3, 3), (2, 0), (0, 2), (1, 0)),
    ((0, 0), (3, 0), (0, 1), (0, 3)),
)
ORDER = (1, 3, 2)
LOG2E = 1.4426950408889634


def kernel(
    len_hbm,
    beh_hbm,
    ids_hbm,
    ids2_hbm,
    cand_hbm,
    wq_hbm,
    wk_hbm,
    wh_hbm,
    bh_hbm,
    wo_hbm,
    out_ref,
    len_ref,
    beh_v,
    ids_ref,
    ids2_ref,
    cand_ref,
    wq_ref,
    wk_ref,
    wh_ref,
    bh_ref,
    wo_ref,
    rhs,
    own16,
    low16,
    acc,
    own,
    s_send,
    add_buf,
    add_send,
    fin_buf,
    cnt_x,
    cnt_xb,
    cnt_y,
    cnt_yb,
    ga,
    gb,
    mine,
    q2,
    wt,
    hc,
    bcol,
    wcol,
    out_send,
    out_buf,
    inv_ref,
    bias_ref,
    sc,
    load_sem,
    op_sem,
    cand_s,
    cnt_s,
    cnt_r,
    rs_s,
    add_r,
    fin_r,
    ag_s,
    ag_r,
    out_s,
):
    s = lax.axis_index("seq")
    c = lax.axis_index("cand")
    x, y = s // NY, s % NY

    pairs = (
        (len_hbm, len_ref),
        (ids_hbm, ids_ref),
        (ids2_hbm, ids2_ref),
        (cand_hbm, cand_ref),
        (wq_hbm, wq_ref),
        (wk_hbm, wk_ref),
        (wh_hbm, wh_ref),
        (bh_hbm, bh_ref),
        (wo_hbm, wo_ref),
    )
    ops = [pltpu.make_async_copy(a, b, op_sem.at[n]) for n, (a, b) in enumerate(pairs)]
    loads = [
        pltpu.make_async_copy(
            beh_hbm.at[0, pl.ds(k * CH, CH), :], beh_v.at[pl.ds(k * CH, CH), :], load_sem.at[k]
        )
        for k in range(CHUNKS)
    ]
    for cp in ops[:3] + loads + ops[3:]:
        cp.start()

    def seq_at(dx, dy):
        return ((x + dx) % NX) * NY + (y + dy) % NY

    barrier = pltpu.get_barrier_semaphore()
    for k in range(1, 16):
        pl.semaphore_signal(
            barrier, inc=1, device_id=(seq_at(k // 4, k % 4), c), device_id_type=pl.DeviceIdType.MESH
        )
    for j in range(1, NCAND):
        pl.semaphore_signal(
            barrier, inc=1, device_id=(s, (c + j) % NCAND), device_id_type=pl.DeviceIdType.MESH
        )

    for cp in ops[:3]:
        cp.wait()
    length = len_ref[0, 0]
    idrow = ids_ref[...]
    live = lax.broadcasted_iota(jnp.int32, (1, SLOTS), 1) < length
    high = (idrow >> 8) & 3
    mid = (idrow >> 6) & 3
    owner_row = jnp.where(idrow >= HALF, mid * 4 + high, high * 4 + mid)
    low_row = jnp.where(live, idrow & (ROWS - 1), 255)
    own16[...] = jnp.broadcast_to(owner_row.astype(F32), (16, SLOTS)).astype(BF16)
    low16[...] = jnp.broadcast_to(low_row.astype(F32), (16, SLOTS)).astype(BF16)
    ahot_row = jnp.where(live, idrow >> 7, 255).astype(F32)
    ids_t = jnp.concatenate([ids2_ref[...], ids2_ref[...]], axis=0).T
    half_t = (ids_t >> 10).astype(F32).astype(BF16)
    low_t = (ids_t & 127).astype(F32).astype(BF16)

    iota16 = lax.broadcasted_iota(jnp.int32, (ROWS, 128), 0).astype(F32).astype(BF16)

    def onehot(owners, k0, kc):
        parts = []
        for dx, dy in owners:
            p16 = jnp.full((16, kc), seq_at(dx, dy).astype(F32), F32).astype(BF16)
            b16 = jnp.where(own16[:, pl.ds(k0, kc)] == p16, low16[:, pl.ds(k0, kc)], BF16(255))
            cols = []
            for t in range(kc // 128):
                bb = jnp.broadcast_to(b16[None, :, t * 128 : (t + 1) * 128], (ROWS // 16, 16, 128))
                cols.append(jnp.where(iota16 == bb.reshape(ROWS, 128), BF16(1), BF16(0)))
            parts.append(jnp.concatenate(cols, axis=1))
        return jnp.concatenate(parts, axis=0)

    def block_sums(i, k0, kc):
        rows = jnp.concatenate([rhs[0, k0 : k0 + kc, :], rhs[1, k0 : k0 + kc, :]], axis=1)
        return [
            jnp.dot(onehot(owners, k0, kc), rows, preferred_element_type=F32)
            for owners in (SETS[i][:2], SETS[i][2:])
        ]

    def put_sums(i, n, val):
        for half in range(2):
            s_send[half, i, n * 2 * ROWS : (n + 1) * 2 * ROWS, :] = val[
                :, half * D : (half + 1) * D
            ].astype(BF16)

    lane = lax.broadcasted_iota(jnp.int32, (128, 128), 1).astype(F32).astype(BF16)
    a_iota = lax.broadcasted_iota(jnp.int32, (16, CH), 0).astype(F32).astype(BF16)
    zero = BF16(0)
    counts = jnp.zeros((16, 128), F32)
    for k in range(CHUNKS):
        loads[k].wait()
        bh = []
        for g in range(k * (CH // 128), (k + 1) * (CH // 128)):
            upper = jnp.broadcast_to(half_t[:, g : g + 1], (128, 128)) != zero
            v = beh_v[g * 128 : (g + 1) * 128, :].astype(BF16)
            rhs[0, g * 128 : (g + 1) * 128, :] = jnp.where(upper, zero, v)
            rhs[1, g * 128 : (g + 1) * 128, :] = jnp.where(upper, v, zero)
            low = jnp.broadcast_to(low_t[:, g : g + 1], (128, 128))
            bh.append(jnp.where(low == lane, BF16(1), zero))
        ab = jnp.broadcast_to(ahot_row[:, k * CH : (k + 1) * CH], (16, CH)).astype(BF16)
        ah = jnp.where(ab == a_iota, BF16(1), zero)
        counts = counts + jnp.dot(ah, jnp.concatenate(bh, axis=0), preferred_element_type=F32)
        for n, part in enumerate(block_sums(0, k * CH, CH)):
            if k == 0:
                acc[n] = part
            else:
                acc[n] += part
    for n in range(2):
        put_sums(0, n, acc[n])
    cnt_x[...] = counts

    def flip(half, p, q):
        return (q, p) if half else (p, q)

    def rs_start(i):
        for j, offset in enumerate(SETS[i]):
            for half in range(2):
                p, q = flip(half, *offset)
                src = s_send.at[half, i, pl.ds(j * ROWS, ROWS), :]
                if p and q:
                    remote(
                        src,
                        add_buf.at[half, p - 1, q - 1],
                        rs_s.at[0],
                        add_r.at[half * 3 + p - 1],
                        (seq_at(*flip(half, 0, q)), c),
                    ).start()
                elif q:
                    dst = fin_buf.at[half, q - 1]
                    remote(
                        src, dst, rs_s.at[1], fin_r.at[half], (seq_at(*offset), c)
                    ).start()

    def add_and_send():
        for p in (2, 1, 3):
            for half in range(2):
                wait_bytes(add_buf.at[half, p - 1], add_r.at[half * 3 + p - 1])
                offset = flip(half, p, 0)
                i, j = next((i, z.index(offset)) for i, z in enumerate(SETS) if offset in z)
                val = s_send[half, i, j * ROWS : (j + 1) * ROWS, :].astype(F32)
                for q in range(3):
                    val = val + add_buf[half, p - 1, q].astype(F32)
                add_send[half, p - 1] = val.astype(BF16)
            for half in range(2):
                remote(
                    add_send.at[half, p - 1],
                    fin_buf.at[half, 2 + p],
                    rs_s.at[1],
                    fin_r.at[half],
                    (seq_at(*flip(half, p, 0)), c),
                ).start()

    def cntx_copy(d):
        return remote(cnt_x, cnt_xb.at[d], cnt_s.at[0], cnt_r.at[0], (seq_at(d, 0), c))

    def cnty_copy(d):
        return remote(cnt_y, cnt_yb.at[d], cnt_s.at[1], cnt_r.at[1], (seq_at(0, d), c))

    ops[3].wait()
    pl.semaphore_wait(barrier, 22)
    for d in ORDER:
        cntx_copy(d).start()
    rs_start(0)
    for j in range(1, NCAND):
        peer = (c + j) % NCAND
        remote(cand_ref.at[peer], mine.at[c], cand_s.at[0], cand_s.at[1], (s, peer)).start()
    mine[c] = cand_ref[c]

    for i in range(1, 4):
        val = block_sums(i, 0, SLOTS)
        for n in range(2):
            put_sums(i, n, val[n])
        if i == 3:
            own[...] = val[0][:ROWS]
        rs_start(i)
    add_and_send()

    for cp in ops[4:]:
        cp.wait()
    wait_bytes(mine.at[pl.ds(0, 7)], cand_s.at[1])
    cands = mine[...].reshape(256, 128)
    q = jnp.dot(cands, wq_ref[...], preferred_element_type=F32).astype(BF16)
    q2[...] = (nt_dot(q, wk_ref[...]) * (LOG2E / D**0.5)).astype(BF16)
    wt[...] = wh_ref[...].astype(F32).T.astype(BF16)
    bcol[...] = jnp.broadcast_to(bh_ref[...], (128, HID)).T
    wcol[...] = jnp.broadcast_to(wo_ref[...], (128, HID)).T
    hc[...] = nt_dot(wt[:, :D], cands) + jnp.concatenate([bcol[...], bcol[...]], axis=1)
    wait_bytes(cnt_xb.at[pl.ds(1, 3)], cnt_r.at[0])
    cnt_y[...] = cnt_x[...] + cnt_xb[1] + cnt_xb[2] + cnt_xb[3]

    halves = []
    for half in range(2):
        total = own[:, half * D : (half + 1) * D]
        wait_bytes(fin_buf.at[half], fin_r.at[half])
        for k in range(6):
            total = total + fin_buf[half, k].astype(F32)
        halves.append(total)

    gs = (ga, gb)

    def at_rows(half, px, py):
        p = py * NX + px if half else px * NY + py
        return gs[half].at[pl.ds(pl.multiple_of(p * ROWS, ROWS), ROWS), :]

    for half in range(2):
        at_rows(half, x, y)[...] = halves[half].astype(BF16)

    def ag_copy(half, via, p, q):
        blk = at_rows(half, *[(z + 4 - w) % 4 for z, w in zip((x, y), flip(half, via, 0))])
        n = half * 6 + ((0, 1, 2, 1)[p] if p == 0 or q else 2 + p)
        dev = seq_at(*flip(half, p - via, q))
        return remote(blk, blk, ag_s.at[half], ag_r.at[n], (dev, c))

    for p in ORDER:
        for half in range(2):
            ag_copy(half, 0, p, 0).start()
    first = c % 2 == 0

    def far(relayed):
        for p, q in ((1, 2), (3, 2), (2, 1), (2, 3), (1, 1), (1, 3), (3, 1), (3, 3)):
            for half in range(2):
                if not relayed:
                    ag_copy(half, 0, p, q).start()
                elif relayed == p:
                    ag_copy(half, p, p, q).start()

    for half in range(2):
        ag_copy(half, 0, 2, 2).start()
    pl.when(first)(lambda: far(0))
    for q in (2, 1, 3):
        for half in range(2):
            ag_copy(half, 0, 0, q).start()
    for d in ORDER:
        cnty_copy(d).start()
    for p in (1, 3):
        for half in range(2):
            ag_copy(half, 0, p, 0).wait_recv()
        pl.when(jnp.logical_not(first))(lambda p=p: far(p))
    for half in range(2):
        ag_copy(half, 0, 2, 0).wait_recv()
    pl.when(jnp.logical_not(first))(lambda: far(2))
    wait_bytes(cnt_yb.at[pl.ds(1, 3)], cnt_r.at[1])
    tot = cnt_y[...] + cnt_yb[1] + cnt_yb[2] + cnt_yb[3]
    inv = 1.0 / jnp.maximum(tot, 1.0)
    bias = jnp.where(tot > 0, jnp.log(1.0 + tot), F32(-1e9)).astype(BF16).astype(F32)
    inv_ref[...] = inv
    bias_ref[...] = bias * LOG2E

    for step in range(3):
        for half in range(2):
            size = (3, 6, 3)[step] * ROWS
            wait_bytes(gs[half].at[pl.ds(0, size), :], ag_r.at[half * 6 + step])
    atts = []
    for m in range(2):
        part = slice(m * 128, (m + 1) * 128)
        top = None
        for half in range(2):
            for n in range(4):
                raw = nt_dot(q2[part, :], gs[half][n * MB : (n + 1) * MB, :])
                for j in range(2):
                    r = half * 8 + n * 2 + j
                    t = raw[:, j * 128 : (j + 1) * 128] * inv_ref[r : r + 1, :]
                    t = t + bias_ref[r : r + 1, :]
                    sc[part, r * 128 : (r + 1) * 128] = t
                    top = t if top is None else jnp.maximum(top, t)
        top = jnp.broadcast_to(jnp.max(top, axis=1, keepdims=True), (128, 128))
        att = den = None
        for half in range(2):
            for n in range(4):
                ps = []
                for j in range(2):
                    r = half * 8 + n * 2 + j
                    e = jnp.exp2(sc[part, r * 128 : (r + 1) * 128] - top)
                    den = e if den is None else den + e
                    ps.append((e * inv_ref[r : r + 1, :]).astype(BF16))
                kb = gs[half][n * MB : (n + 1) * MB, :]
                pv = jnp.dot(jnp.concatenate(ps, axis=1), kb, preferred_element_type=F32)
                att = pv if att is None else att + pv
        atts.append((att / jnp.sum(den, axis=1, keepdims=True)).astype(BF16))
    att = jnp.concatenate(atts, axis=0)

    row = 0.0
    for k in range(2):
        part = slice(k * (HID // 2), (k + 1) * (HID // 2))
        hid = jnp.maximum(hc[part, :] + nt_dot(wt[part, D:], att), 0.0)
        hid = hid * jnp.concatenate([wcol[part, :], wcol[part, :]], axis=1)
        row = row + jnp.sum(hid, axis=0, keepdims=True)
    for j in range(NCAND):
        out_send[j, :, :32] = row[:, j * 32 : (j + 1) * 32]
    for j in range(1, NCAND):
        peer = (c + j) % NCAND
        remote(out_send.at[peer], out_buf.at[c], out_s.at[0], out_s.at[1], (s, peer)).start()
    out_buf[c] = out_send[c]
    wait_bytes(mine.at[pl.ds(0, 7)], cand_s.at[0])
    wait_bytes(cnt_xb.at[pl.ds(1, 3)], cnt_s.at[0])
    wait_bytes(cnt_yb.at[pl.ds(1, 3)], cnt_s.at[1])
    wait_bytes(add_buf, rs_s.at[0])
    wait_bytes(fin_buf, rs_s.at[1])
    for half in range(2):
        wait_bytes(gs[half].at[pl.ds(0, 15 * ROWS), :], ag_s.at[half])
    wait_bytes(out_buf.at[pl.ds(0, 7)], out_s.at[0])
    wait_bytes(out_buf.at[pl.ds(0, 7)], out_s.at[1])
    out_ref[...] = out_buf[:, 0, :32]


def on_device(
    behaviors, cluster_ids, lengths, candidates, w_query, w_key, w_hidden, b_hidden, w_out
):
    vmem = pl.BlockSpec(memory_space=pltpu.VMEM)
    dma = pltpu.SemaphoreType.DMA
    return pl.pallas_call(
        kernel,
        out_shape=pltpu.VMEM((8, 32), F32),
        in_specs=[pl.BlockSpec(memory_space=pltpu.HBM)] * 10,
        out_specs=vmem,
        scratch_shapes=[
            pltpu.SMEM((1, 1), jnp.int32),
            pltpu.VMEM((SLOTS, D), F32),
            pltpu.VMEM((1, SLOTS), jnp.int32),
            pltpu.VMEM((64, 128), jnp.int32),
            pltpu.VMEM((8, 32, D), BF16),
            pltpu.VMEM((D, D), BF16),
            pltpu.VMEM((D, D), BF16),
            pltpu.VMEM((2 * D, HID), BF16),
            pltpu.VMEM((1, HID), F32),
            pltpu.VMEM((1, HID), F32),
            pltpu.VMEM((2, SLOTS, D), BF16),
            pltpu.VMEM((16, SLOTS), BF16),
            pltpu.VMEM((16, SLOTS), BF16),
            pltpu.VMEM((2, 2 * ROWS, 2 * D), F32),
            pltpu.VMEM((ROWS, 2 * D), F32),
            pltpu.VMEM((2, 4, MB, D), BF16),
            pltpu.VMEM((2, 3, 3, ROWS, D), BF16),
            pltpu.VMEM((2, 3, ROWS, D), BF16),
            pltpu.VMEM((2, 6, ROWS, D), BF16),
            pltpu.VMEM((16, 128), F32),
            pltpu.VMEM((4, 16, 128), F32),
            pltpu.VMEM((16, 128), F32),
            pltpu.VMEM((4, 16, 128), F32),
            pltpu.VMEM((HALF, D), BF16),
            pltpu.VMEM((HALF, D), BF16),
            pltpu.VMEM((8, 32, D), BF16),
            pltpu.VMEM((256, D), BF16),
            pltpu.VMEM((HID, 2 * D), BF16),
            pltpu.VMEM((HID, 256), F32),
            pltpu.VMEM((HID, 128), F32),
            pltpu.VMEM((HID, 128), F32),
            pltpu.VMEM((8, 1, 128), F32),
            pltpu.VMEM((8, 1, 128), F32),
            pltpu.VMEM((16, 128), F32),
            pltpu.VMEM((16, 128), F32),
            pltpu.VMEM((256, 2048), F32),
            dma((CHUNKS,)),
            dma((9,)),
            dma((2,)),
            dma((2,)),
            dma((2,)),
            dma((2,)),
            dma((6,)),
            dma((2,)),
            dma((2,)),
            dma((12,)),
            dma((2,)),
        ],
        compiler_params=pltpu.CompilerParams(collective_id=0, has_side_effects=True),
        name="fused",
    )(
        lengths,
        behaviors,
        cluster_ids,
        cluster_ids.reshape(64, 128),
        candidates,
        w_query,
        w_key,
        w_hidden,
        b_hidden.reshape(1, HID),
        w_out.reshape(1, HID),
    )


def solution(mesh):
    in_specs = (
        P("cand", "seq", None),
        P("cand", "seq"),
        P("cand", "seq"),
        P(None, ("seq", "cand"), None),
        P(),
        P(),
        P(),
        P(),
        P(),
    )
    return jax.shard_map(
        on_device,
        mesh=mesh,
        in_specs=in_specs,
        out_specs=P(None, ("seq", "cand")),
        check_vma=False,
    )
```

```python
import jax
import jax.numpy as jnp
from jax import lax
from jax.experimental import pallas as pl
from jax.experimental.pallas import tpu as pltpu
from jax.sharding import PartitionSpec as P

BF16 = jnp.bfloat16
F32 = jnp.float32
NX, NY, NCAND = 4, 4, 8
SLOTS, D, HID = 8192, 128, 512
HALF = 1024
CHUNKS = 4
CH = SLOTS // CHUNKS
MB = 256
ROWS = HALF // 16


def remote(src, dst, send, recv, device_id):
    return pltpu.make_async_remote_copy(
        src_ref=src,
        dst_ref=dst,
        send_sem=send,
        recv_sem=recv,
        device_id=device_id,
        device_id_type=pl.DeviceIdType.MESH,
    )


def wait_bytes(ref, sem):
    pltpu.make_async_copy(ref, ref, sem).wait()


def nt_dot(a, b):
    return lax.dot_general(a, b, (((1,), (1,)), ((), ())), preferred_element_type=F32)


SETS = (
    ((2, 2), (2, 1), (2, 3), (1, 2)),
    ((3, 2), (1, 1), (1, 3), (3, 1)),
    ((3, 3), (2, 0), (0, 2), (1, 0)),
    ((0, 0), (3, 0), (0, 1), (0, 3)),
)
ORDER = (1, 3, 2)


def kernel(
    len_hbm,
    beh_hbm,
    ids_hbm,
    ids2_hbm,
    cand_hbm,
    wq_hbm,
    wk_hbm,
    wh_hbm,
    bh_hbm,
    wo_hbm,
    out_ref,
    len_ref,
    beh_v,
    ids_ref,
    ids2_ref,
    cand_ref,
    wq_ref,
    wk_ref,
    wh_ref,
    bh_ref,
    wo_ref,
    rhs,
    own16,
    low16,
    acc,
    own,
    s_send,
    add_buf,
    add_send,
    fin_buf,
    cnt_x,
    cnt_xb,
    cnt_y,
    cnt_yb,
    ga,
    gb,
    mine,
    q2,
    wt,
    hc,
    bcol,
    wcol,
    out_send,
    out_buf,
    inv_ref,
    mult_ref,
    bias_ref,
    sc,
    load_sem,
    op_sem,
    cand_s,
    cnt_s,
    cnt_r,
    rs_s,
    add_r,
    fin_r,
    ag_s,
    ag_r,
    out_s,
):
    s = lax.axis_index("seq")
    c = lax.axis_index("cand")
    x, y = s // NY, s % NY

    pairs = (
        (len_hbm, len_ref),
        (ids_hbm, ids_ref),
        (ids2_hbm, ids2_ref),
        (cand_hbm, cand_ref),
        (wq_hbm, wq_ref),
        (wk_hbm, wk_ref),
        (wh_hbm, wh_ref),
        (bh_hbm, bh_ref),
        (wo_hbm, wo_ref),
    )
    ops = [pltpu.make_async_copy(a, b, op_sem.at[n]) for n, (a, b) in enumerate(pairs)]
    loads = [
        pltpu.make_async_copy(
            beh_hbm.at[0, pl.ds(k * CH, CH), :], beh_v.at[pl.ds(k * CH, CH), :], load_sem.at[k]
        )
        for k in range(CHUNKS)
    ]
    for cp in ops[:3] + loads + ops[3:]:
        cp.start()

    def seq_at(dx, dy):
        return ((x + dx) % NX) * NY + (y + dy) % NY

    barrier = pltpu.get_barrier_semaphore()
    for k in range(1, 16):
        pl.semaphore_signal(
            barrier, inc=1, device_id=(seq_at(k // 4, k % 4), c), device_id_type=pl.DeviceIdType.MESH
        )
    for j in range(1, NCAND):
        pl.semaphore_signal(
            barrier, inc=1, device_id=(s, (c + j) % NCAND), device_id_type=pl.DeviceIdType.MESH
        )

    for cp in ops[:3]:
        cp.wait()
    length = len_ref[0, 0]
    idrow = ids_ref[...]
    live = lax.broadcasted_iota(jnp.int32, (1, SLOTS), 1) < length
    high = (idrow >> 8) & 3
    mid = (idrow >> 6) & 3
    owner_row = jnp.where(idrow >= HALF, mid * 4 + high, high * 4 + mid)
    low_row = jnp.where(live, idrow & (ROWS - 1), 255)
    own16[...] = jnp.broadcast_to(owner_row.astype(F32), (16, SLOTS)).astype(BF16)
    low16[...] = jnp.broadcast_to(low_row.astype(F32), (16, SLOTS)).astype(BF16)
    ahot_row = jnp.where(live, idrow >> 7, 255).astype(F32)
    ids_t = jnp.concatenate([ids2_ref[...], ids2_ref[...]], axis=0).T
    half_t = (ids_t >> 10).astype(F32).astype(BF16)
    low_t = (ids_t & 127).astype(F32).astype(BF16)

    iota16 = lax.broadcasted_iota(jnp.int32, (ROWS, 128), 0).astype(F32).astype(BF16)

    def onehot(owners, k0, kc):
        parts = []
        for dx, dy in owners:
            p16 = jnp.full((16, kc), seq_at(dx, dy).astype(F32), F32).astype(BF16)
            b16 = jnp.where(own16[:, pl.ds(k0, kc)] == p16, low16[:, pl.ds(k0, kc)], BF16(255))
            cols = []
            for t in range(kc // 128):
                bb = jnp.broadcast_to(b16[None, :, t * 128 : (t + 1) * 128], (ROWS // 16, 16, 128))
                cols.append(jnp.where(iota16 == bb.reshape(ROWS, 128), BF16(1), BF16(0)))
            parts.append(jnp.concatenate(cols, axis=1))
        return jnp.concatenate(parts, axis=0)

    def block_sums(i, k0, kc):
        rows = jnp.concatenate([rhs[0, k0 : k0 + kc, :], rhs[1, k0 : k0 + kc, :]], axis=1)
        return [
            jnp.dot(onehot(owners, k0, kc), rows, preferred_element_type=F32)
            for owners in (SETS[i][:2], SETS[i][2:])
        ]

    def put_sums(i, n, val):
        for half in range(2):
            s_send[half, i, n * 2 * ROWS : (n + 1) * 2 * ROWS, :] = val[
                :, half * D : (half + 1) * D
            ].astype(BF16)

    lane = lax.broadcasted_iota(jnp.int32, (128, 128), 1).astype(F32).astype(BF16)
    a_iota = lax.broadcasted_iota(jnp.int32, (16, CH), 0).astype(F32).astype(BF16)
    zero = BF16(0)
    counts = jnp.zeros((16, 128), F32)
    for k in range(CHUNKS):
        loads[k].wait()
        bh = []
        for g in range(k * (CH // 128), (k + 1) * (CH // 128)):
            upper = jnp.broadcast_to(half_t[:, g : g + 1], (128, 128)) != zero
            v = beh_v[g * 128 : (g + 1) * 128, :].astype(BF16)
            rhs[0, g * 128 : (g + 1) * 128, :] = jnp.where(upper, zero, v)
            rhs[1, g * 128 : (g + 1) * 128, :] = jnp.where(upper, v, zero)
            low = jnp.broadcast_to(low_t[:, g : g + 1], (128, 128))
            bh.append(jnp.where(low == lane, BF16(1), zero))
        ab = jnp.broadcast_to(ahot_row[:, k * CH : (k + 1) * CH], (16, CH)).astype(BF16)
        ah = jnp.where(ab == a_iota, BF16(1), zero)
        counts = counts + jnp.dot(ah, jnp.concatenate(bh, axis=0), preferred_element_type=F32)
        for n, part in enumerate(block_sums(0, k * CH, CH)):
            if k == 0:
                acc[n] = part
            else:
                acc[n] += part
    for n in range(2):
        put_sums(0, n, acc[n])
    cnt_x[...] = counts

    def flip(half, p, q):
        return (q, p) if half else (p, q)

    def rs_start(i):
        for j, offset in enumerate(SETS[i]):
            for half in range(2):
                p, q = flip(half, *offset)
                src = s_send.at[half, i, pl.ds(j * ROWS, ROWS), :]
                if p and q:
                    remote(
                        src,
                        add_buf.at[half, p - 1, q - 1],
                        rs_s.at[0],
                        add_r.at[half * 3 + p - 1],
                        (seq_at(*flip(half, 0, q)), c),
                    ).start()
                elif q:
                    dst = fin_buf.at[half, q - 1]
                    remote(
                        src, dst, rs_s.at[1], fin_r.at[half], (seq_at(*offset), c)
                    ).start()

    def add_and_send():
        for p in (2, 1, 3):
            for half in range(2):
                wait_bytes(add_buf.at[half, p - 1], add_r.at[half * 3 + p - 1])
                offset = flip(half, p, 0)
                i, j = next((i, z.index(offset)) for i, z in enumerate(SETS) if offset in z)
                val = s_send[half, i, j * ROWS : (j + 1) * ROWS, :].astype(F32)
                for q in range(3):
                    val = val + add_buf[half, p - 1, q].astype(F32)
                add_send[half, p - 1] = val.astype(BF16)
            for half in range(2):
                remote(
                    add_send.at[half, p - 1],
                    fin_buf.at[half, 2 + p],
                    rs_s.at[1],
                    fin_r.at[half],
                    (seq_at(*flip(half, p, 0)), c),
                ).start()

    def cntx_copy(d):
        return remote(cnt_x, cnt_xb.at[d], cnt_s.at[0], cnt_r.at[0], (seq_at(d, 0), c))

    def cnty_copy(d):
        return remote(cnt_y, cnt_yb.at[d], cnt_s.at[1], cnt_r.at[1], (seq_at(0, d), c))

    ops[3].wait()
    pl.semaphore_wait(barrier, 22)
    rs_start(0)
    for j in range(1, NCAND):
        peer = (c + j) % NCAND
        remote(cand_ref.at[peer], mine.at[c], cand_s.at[0], cand_s.at[1], (s, peer)).start()
    mine[c] = cand_ref[c]

    for i in range(1, 4):
        val = block_sums(i, 0, SLOTS)
        for n in range(2):
            put_sums(i, n, val[n])
        if i == 3:
            own[...] = val[0][:ROWS]
        rs_start(i)
        if i == 1:
            for d in ORDER:
                cntx_copy(d).start()
    add_and_send()

    for cp in ops[4:]:
        cp.wait()
    wait_bytes(mine.at[pl.ds(0, 7)], cand_s.at[1])
    cands = mine[...].reshape(256, 128)
    q = jnp.dot(cands, wq_ref[...], preferred_element_type=F32).astype(BF16)
    q2[...] = nt_dot(q, wk_ref[...]).astype(BF16)
    wt[...] = wh_ref[...].astype(F32).T.astype(BF16)
    bcol[...] = jnp.broadcast_to(bh_ref[...], (128, HID)).T
    wcol[...] = jnp.broadcast_to(wo_ref[...], (128, HID)).T
    hc[...] = nt_dot(wt[:, :D], cands) + jnp.concatenate([bcol[...], bcol[...]], axis=1)
    wait_bytes(cnt_xb.at[pl.ds(1, 3)], cnt_r.at[0])
    cnt_y[...] = cnt_x[...] + cnt_xb[1] + cnt_xb[2] + cnt_xb[3]

    halves = []
    for half in range(2):
        total = own[:, half * D : (half + 1) * D]
        wait_bytes(fin_buf.at[half], fin_r.at[half])
        for k in range(6):
            total = total + fin_buf[half, k].astype(F32)
        halves.append(total)

    gs = (ga, gb)

    def at_rows(half, px, py):
        p = py * NX + px if half else px * NY + py
        return gs[half].at[pl.ds(pl.multiple_of(p * ROWS, ROWS), ROWS), :]

    for half in range(2):
        at_rows(half, x, y)[...] = halves[half].astype(BF16)

    def ag_copy(half, via, p, q):
        blk = at_rows(half, *[(z + 4 - w) % 4 for z, w in zip((x, y), flip(half, via, 0))])
        n = half * 6 + ((0, 1, 2, 1)[p] if p == 0 or q else 2 + p)
        dev = seq_at(*flip(half, p - via, q))
        return remote(blk, blk, ag_s.at[half], ag_r.at[n], (dev, c))

    for p in ORDER:
        for half in range(2):
            ag_copy(half, 0, p, 0).start()
    first = c % 2 == 0

    def far(relayed):
        for p, q in ((1, 2), (3, 2), (2, 1), (2, 3)):
            for half in range(2):
                if not relayed:
                    ag_copy(half, 0, p, q).start()
                elif relayed == p:
                    ag_copy(half, p, p, q).start()

    for half in range(2):
        ag_copy(half, 0, 2, 2).start()
    pl.when(first)(lambda: far(0))
    for q in (2, 1, 3):
        for half in range(2):
            ag_copy(half, 0, 0, q).start()
    for d in ORDER:
        cnty_copy(d).start()
    for p in (1, 3):
        for half in range(2):
            ag_copy(half, 0, p, 0).wait_recv()
            for q in (1, 3):
                ag_copy(half, p, p, q).start()
        pl.when(jnp.logical_not(first))(lambda p=p: far(p))
    for half in range(2):
        ag_copy(half, 0, 2, 0).wait_recv()
    pl.when(jnp.logical_not(first))(lambda: far(2))
    wait_bytes(cnt_yb.at[pl.ds(1, 3)], cnt_r.at[1])
    tot = cnt_y[...] + cnt_yb[1] + cnt_yb[2] + cnt_yb[3]
    inv = 1.0 / jnp.maximum(tot, 1.0)
    inv_ref[...] = inv
    mult_ref[...] = inv * (1.0 / jnp.sqrt(F32(D)))
    bias_ref[...] = (
        jnp.where(tot > 0, jnp.log(1.0 + tot), F32(-1e9)).astype(BF16).astype(F32)
    )

    top = den = att = None
    for step, dists in ((0, (0,)), (2, (2,)), (1, (1, 3))):
        keys, rows = [], []
        for half in range(2):
            size = (3, 6, 3)[step] * ROWS
            wait_bytes(gs[half].at[pl.ds(0, size), :], ag_r.at[half * 6 + step])
        for d in dists:
            for half in range(2):
                g = (y + NY - d) % NY if half else (x + NX - d) % NX
                keys.append(gs[half][pl.ds(pl.multiple_of(g * MB, MB), MB), :])
                rows += [half * 8 + g * 2, half * 8 + g * 2 + 1]
        new = None
        for n, kb in enumerate(keys):
            raw = nt_dot(q2[...], kb)
            for j in range(2):
                r = rows[2 * n + j]
                t = raw[:, j * 128 : (j + 1) * 128] * mult_ref[pl.ds(r, 1), :]
                t = t + bias_ref[pl.ds(r, 1), :]
                sc[:, (2 * n + j) * 128 : (2 * n + j + 1) * 128] = t
                new = t if new is None else jnp.maximum(new, t)
        new = jnp.broadcast_to(jnp.max(new, axis=1, keepdims=True), (256, 128))
        if top is not None:
            new = jnp.maximum(top, new)
            alpha = jnp.exp(top - new)
            den = den * alpha
            att = att * alpha
        top = new
        for n, kb in enumerate(keys):
            ps = []
            for j in range(2):
                r = rows[2 * n + j]
                e = jnp.exp(sc[:, (2 * n + j) * 128 : (2 * n + j + 1) * 128] - top)
                den = e if den is None else den + e
                ps.append((e * inv_ref[pl.ds(r, 1), :]).astype(BF16))
            p = jnp.concatenate(ps, axis=1)
            pv = jnp.dot(p, kb, preferred_element_type=F32)
            att = pv if att is None else att + pv
    att = (att / jnp.sum(den, axis=1, keepdims=True)).astype(BF16)

    row = 0.0
    for k in range(2):
        part = slice(k * (HID // 2), (k + 1) * (HID // 2))
        hid = jnp.maximum(hc[part, :] + nt_dot(wt[part, D:], att), 0.0)
        hid = hid * jnp.concatenate([wcol[part, :], wcol[part, :]], axis=1)
        row = row + jnp.sum(hid, axis=0, keepdims=True)
    for j in range(NCAND):
        out_send[j, :, :32] = row[:, j * 32 : (j + 1) * 32]
    for j in range(1, NCAND):
        peer = (c + j) % NCAND
        remote(out_send.at[peer], out_buf.at[c], out_s.at[0], out_s.at[1], (s, peer)).start()
    out_buf[c] = out_send[c]
    wait_bytes(mine.at[pl.ds(0, 7)], cand_s.at[0])
    wait_bytes(cnt_xb.at[pl.ds(1, 3)], cnt_s.at[0])
    wait_bytes(cnt_yb.at[pl.ds(1, 3)], cnt_s.at[1])
    wait_bytes(add_buf, rs_s.at[0])
    wait_bytes(fin_buf, rs_s.at[1])
    for half in range(2):
        wait_bytes(gs[half].at[pl.ds(0, 15 * ROWS), :], ag_s.at[half])
    wait_bytes(out_buf.at[pl.ds(0, 7)], out_s.at[0])
    wait_bytes(out_buf.at[pl.ds(0, 7)], out_s.at[1])
    out_ref[...] = out_buf[:, 0, :32]


def on_device(
    behaviors, cluster_ids, lengths, candidates, w_query, w_key, w_hidden, b_hidden, w_out
):
    vmem = pl.BlockSpec(memory_space=pltpu.VMEM)
    dma = pltpu.SemaphoreType.DMA
    return pl.pallas_call(
        kernel,
        out_shape=pltpu.VMEM((8, 32), F32),
        in_specs=[pl.BlockSpec(memory_space=pltpu.HBM)] * 10,
        out_specs=vmem,
        scratch_shapes=[
            pltpu.SMEM((1, 1), jnp.int32),
            pltpu.VMEM((SLOTS, D), F32),
            pltpu.VMEM((1, SLOTS), jnp.int32),
            pltpu.VMEM((64, 128), jnp.int32),
            pltpu.VMEM((8, 32, D), BF16),
            pltpu.VMEM((D, D), BF16),
            pltpu.VMEM((D, D), BF16),
            pltpu.VMEM((2 * D, HID), BF16),
            pltpu.VMEM((1, HID), F32),
            pltpu.VMEM((1, HID), F32),
            pltpu.VMEM((2, SLOTS, D), BF16),
            pltpu.VMEM((16, SLOTS), BF16),
            pltpu.VMEM((16, SLOTS), BF16),
            pltpu.VMEM((2, 2 * ROWS, 2 * D), F32),
            pltpu.VMEM((ROWS, 2 * D), F32),
            pltpu.VMEM((2, 4, MB, D), BF16),
            pltpu.VMEM((2, 3, 3, ROWS, D), BF16),
            pltpu.VMEM((2, 3, ROWS, D), BF16),
            pltpu.VMEM((2, 6, ROWS, D), BF16),
            pltpu.VMEM((16, 128), F32),
            pltpu.VMEM((4, 16, 128), F32),
            pltpu.VMEM((16, 128), F32),
            pltpu.VMEM((4, 16, 128), F32),
            pltpu.VMEM((HALF, D), BF16),
            pltpu.VMEM((HALF, D), BF16),
            pltpu.VMEM((8, 32, D), BF16),
            pltpu.VMEM((256, D), BF16),
            pltpu.VMEM((HID, 2 * D), BF16),
            pltpu.VMEM((HID, 256), F32),
            pltpu.VMEM((HID, 128), F32),
            pltpu.VMEM((HID, 128), F32),
            pltpu.VMEM((8, 1, 128), F32),
            pltpu.VMEM((8, 1, 128), F32),
            pltpu.VMEM((16, 128), F32),
            pltpu.VMEM((16, 128), F32),
            pltpu.VMEM((16, 128), F32),
            pltpu.VMEM((256, 1024), F32),
            dma((CHUNKS,)),
            dma((9,)),
            dma((2,)),
            dma((2,)),
            dma((2,)),
            dma((2,)),
            dma((6,)),
            dma((2,)),
            dma((2,)),
            dma((12,)),
            dma((2,)),
        ],
        compiler_params=pltpu.CompilerParams(collective_id=0, has_side_effects=True),
        name="fused",
    )(
        lengths,
        behaviors,
        cluster_ids,
        cluster_ids.reshape(64, 128),
        candidates,
        w_query,
        w_key,
        w_hidden,
        b_hidden.reshape(1, HID),
        w_out.reshape(1, HID),
    )


def solution(mesh):
    in_specs = (
        P("cand", "seq", None),
        P("cand", "seq"),
        P("cand", "seq"),
        P(None, ("seq", "cand"), None),
        P(),
        P(),
        P(),
        P(),
        P(),
    )
    return jax.shard_map(
        on_device,
        mesh=mesh,
        in_specs=in_specs,
        out_specs=P(None, ("seq", "cand")),
        check_vma=False,
    )
```

```python
import jax
import jax.numpy as jnp
from jax import lax
from jax.experimental import pallas as pl
from jax.experimental.pallas import tpu as pltpu
from jax.sharding import PartitionSpec as P

BF16 = jnp.bfloat16
F32 = jnp.float32
NX, NY, NCAND = 4, 4, 8
SLOTS, D, HID = 8192, 128, 512
HALF = 1024
CHUNKS = 4
CH = SLOTS // CHUNKS
MB = 256
ROWS = HALF // 16


def remote(src, dst, send, recv, device_id):
    return pltpu.make_async_remote_copy(
        src_ref=src,
        dst_ref=dst,
        send_sem=send,
        recv_sem=recv,
        device_id=device_id,
        device_id_type=pl.DeviceIdType.MESH,
    )


def wait_bytes(ref, sem):
    pltpu.make_async_copy(ref, ref, sem).wait()


def nt_dot(a, b):
    return lax.dot_general(a, b, (((1,), (1,)), ((), ())), preferred_element_type=F32)


SETS = (
    ((2, 2), (2, 1), (2, 3), (1, 2)),
    ((3, 2), (1, 1), (1, 3), (3, 1)),
    ((3, 3), (2, 0), (0, 2), (1, 0)),
    ((0, 0), (3, 0), (0, 1), (0, 3)),
)
ORDER = (1, 3, 2)
LOG2E = 1.4426950408889634


def kernel(
    len_hbm,
    beh_hbm,
    ids_hbm,
    ids2_hbm,
    cand_hbm,
    wq_hbm,
    wk_hbm,
    wh_hbm,
    bh_hbm,
    wo_hbm,
    out_ref,
    len_ref,
    beh_v,
    ids_ref,
    ids2_ref,
    cand_ref,
    wq_ref,
    wk_ref,
    wh_ref,
    bh_ref,
    wo_ref,
    rhs,
    own16,
    low16,
    acc,
    own,
    s_send,
    add_buf,
    add_send,
    fin_buf,
    cnt_x,
    cnt_xb,
    cnt_y,
    cnt_yb,
    ga,
    gb,
    mine,
    q2,
    wt,
    hc,
    bcol,
    wcol,
    out_send,
    out_buf,
    inv_ref,
    bias_ref,
    sc,
    load_sem,
    op_sem,
    cand_s,
    cnt_s,
    cnt_r,
    rs_s,
    add_r,
    fin_r,
    ag_s,
    ag_r,
    out_s,
):
    s = lax.axis_index("seq")
    c = lax.axis_index("cand")
    x, y = s // NY, s % NY

    pairs = (
        (len_hbm, len_ref),
        (ids_hbm, ids_ref),
        (ids2_hbm, ids2_ref),
        (cand_hbm, cand_ref),
        (wq_hbm, wq_ref),
        (wk_hbm, wk_ref),
        (wh_hbm, wh_ref),
        (bh_hbm, bh_ref),
        (wo_hbm, wo_ref),
    )
    ops = [pltpu.make_async_copy(a, b, op_sem.at[n]) for n, (a, b) in enumerate(pairs)]
    loads = [
        pltpu.make_async_copy(
            beh_hbm.at[0, pl.ds(k * CH, CH), :], beh_v.at[pl.ds(k * CH, CH), :], load_sem.at[k]
        )
        for k in range(CHUNKS)
    ]
    for cp in ops[:3] + loads + ops[3:]:
        cp.start()

    def seq_at(dx, dy):
        return ((x + dx) % NX) * NY + (y + dy) % NY

    barrier = pltpu.get_barrier_semaphore()
    for k in range(1, 16):
        pl.semaphore_signal(
            barrier, inc=1, device_id=(seq_at(k // 4, k % 4), c), device_id_type=pl.DeviceIdType.MESH
        )
    for j in range(1, NCAND):
        pl.semaphore_signal(
            barrier, inc=1, device_id=(s, (c + j) % NCAND), device_id_type=pl.DeviceIdType.MESH
        )

    for cp in ops[:3]:
        cp.wait()
    length = len_ref[0, 0]
    idrow = ids_ref[...]
    live = lax.broadcasted_iota(jnp.int32, (1, SLOTS), 1) < length
    high = (idrow >> 8) & 3
    mid = (idrow >> 6) & 3
    owner_row = jnp.where(idrow >= HALF, mid * 4 + high, high * 4 + mid)
    low_row = jnp.where(live, idrow & (ROWS - 1), 255)
    own16[...] = jnp.broadcast_to(owner_row.astype(F32), (16, SLOTS)).astype(BF16)
    low16[...] = jnp.broadcast_to(low_row.astype(F32), (16, SLOTS)).astype(BF16)
    ahot_row = jnp.where(live, idrow >> 7, 255).astype(F32)
    ids_t = jnp.concatenate([ids2_ref[...], ids2_ref[...]], axis=0).T
    half_t = (ids_t >> 10).astype(F32).astype(BF16)
    low_t = (ids_t & 127).astype(F32).astype(BF16)

    iota16 = lax.broadcasted_iota(jnp.int32, (ROWS, 128), 0).astype(F32).astype(BF16)

    def onehot(owners, k0, kc):
        parts = []
        for dx, dy in owners:
            p16 = jnp.full((16, kc), seq_at(dx, dy).astype(F32), F32).astype(BF16)
            b16 = jnp.where(own16[:, pl.ds(k0, kc)] == p16, low16[:, pl.ds(k0, kc)], BF16(255))
            cols = []
            for t in range(kc // 128):
                bb = jnp.broadcast_to(b16[None, :, t * 128 : (t + 1) * 128], (ROWS // 16, 16, 128))
                cols.append(jnp.where(iota16 == bb.reshape(ROWS, 128), BF16(1), BF16(0)))
            parts.append(jnp.concatenate(cols, axis=1))
        return jnp.concatenate(parts, axis=0)

    def block_sums(i, k0, kc):
        rows = jnp.concatenate([rhs[0, k0 : k0 + kc, :], rhs[1, k0 : k0 + kc, :]], axis=1)
        return [
            jnp.dot(onehot(owners, k0, kc), rows, preferred_element_type=F32)
            for owners in (SETS[i][:2], SETS[i][2:])
        ]

    def put_sums(i, n, val):
        for half in range(2):
            s_send[half, i, n * 2 * ROWS : (n + 1) * 2 * ROWS, :] = val[
                :, half * D : (half + 1) * D
            ].astype(BF16)

    lane = lax.broadcasted_iota(jnp.int32, (128, 128), 1).astype(F32).astype(BF16)
    a_iota = lax.broadcasted_iota(jnp.int32, (16, CH), 0).astype(F32).astype(BF16)
    zero = BF16(0)
    counts = jnp.zeros((16, 128), F32)
    for k in range(CHUNKS):
        loads[k].wait()
        bh = []
        for g in range(k * (CH // 128), (k + 1) * (CH // 128)):
            upper = jnp.broadcast_to(half_t[:, g : g + 1], (128, 128)) != zero
            v = beh_v[g * 128 : (g + 1) * 128, :].astype(BF16)
            rhs[0, g * 128 : (g + 1) * 128, :] = jnp.where(upper, zero, v)
            rhs[1, g * 128 : (g + 1) * 128, :] = jnp.where(upper, v, zero)
            low = jnp.broadcast_to(low_t[:, g : g + 1], (128, 128))
            bh.append(jnp.where(low == lane, BF16(1), zero))
        ab = jnp.broadcast_to(ahot_row[:, k * CH : (k + 1) * CH], (16, CH)).astype(BF16)
        ah = jnp.where(ab == a_iota, BF16(1), zero)
        counts = counts + jnp.dot(ah, jnp.concatenate(bh, axis=0), preferred_element_type=F32)
        for n, part in enumerate(block_sums(0, k * CH, CH)):
            if k == 0:
                acc[n] = part
            else:
                acc[n] += part
    for n in range(2):
        put_sums(0, n, acc[n])
    cnt_x[...] = counts

    def flip(half, p, q):
        return (q, p) if half else (p, q)

    def rs_start(i):
        for j, offset in enumerate(SETS[i]):
            for half in range(2):
                p, q = flip(half, *offset)
                src = s_send.at[half, i, pl.ds(j * ROWS, ROWS), :]
                if p and q:
                    remote(
                        src,
                        add_buf.at[half, p - 1, q - 1],
                        rs_s.at[0],
                        add_r.at[half * 3 + p - 1],
                        (seq_at(*flip(half, 0, q)), c),
                    ).start()
                elif q:
                    dst = fin_buf.at[half, q - 1]
                    remote(
                        src, dst, rs_s.at[1], fin_r.at[half], (seq_at(*offset), c)
                    ).start()

    def add_and_send():
        for p in (2, 1, 3):
            for half in range(2):
                wait_bytes(add_buf.at[half, p - 1], add_r.at[half * 3 + p - 1])
                offset = flip(half, p, 0)
                i, j = next((i, z.index(offset)) for i, z in enumerate(SETS) if offset in z)
                val = s_send[half, i, j * ROWS : (j + 1) * ROWS, :].astype(F32)
                for q in range(3):
                    val = val + add_buf[half, p - 1, q].astype(F32)
                add_send[half, p - 1] = val.astype(BF16)
            for half in range(2):
                remote(
                    add_send.at[half, p - 1],
                    fin_buf.at[half, 2 + p],
                    rs_s.at[1],
                    fin_r.at[half],
                    (seq_at(*flip(half, p, 0)), c),
                ).start()

    def cntx_copy(d):
        return remote(cnt_x, cnt_xb.at[d], cnt_s.at[0], cnt_r.at[0], (seq_at(d, 0), c))

    def cnty_copy(d):
        return remote(cnt_y, cnt_yb.at[d], cnt_s.at[1], cnt_r.at[1], (seq_at(0, d), c))

    ops[3].wait()
    pl.semaphore_wait(barrier, 22)
    for d in ORDER:
        cntx_copy(d).start()
    rs_start(0)
    for j in range(1, NCAND):
        peer = (c + j) % NCAND
        remote(cand_ref.at[peer], mine.at[c], cand_s.at[0], cand_s.at[1], (s, peer)).start()
    mine[c] = cand_ref[c]

    for i in range(1, 4):
        val = block_sums(i, 0, SLOTS)
        for n in range(2):
            put_sums(i, n, val[n])
        if i == 3:
            own[...] = val[0][:ROWS]
        rs_start(i)
    add_and_send()

    for cp in ops[4:]:
        cp.wait()
    wait_bytes(mine.at[pl.ds(0, 7)], cand_s.at[1])
    cands = mine[...].reshape(256, 128)
    q = jnp.dot(cands, wq_ref[...], preferred_element_type=F32).astype(BF16)
    q2[...] = (nt_dot(q, wk_ref[...]) * (LOG2E / D**0.5)).astype(BF16)
    wt[...] = wh_ref[...].astype(F32).T.astype(BF16)
    bcol[...] = jnp.broadcast_to(bh_ref[...], (128, HID)).T
    wcol[...] = jnp.broadcast_to(wo_ref[...], (128, HID)).T
    hc[...] = nt_dot(wt[:, :D], cands) + jnp.concatenate([bcol[...], bcol[...]], axis=1)
    wait_bytes(cnt_xb.at[pl.ds(1, 3)], cnt_r.at[0])
    cnt_y[...] = cnt_x[...] + cnt_xb[1] + cnt_xb[2] + cnt_xb[3]

    halves = []
    for half in range(2):
        total = own[:, half * D : (half + 1) * D]
        wait_bytes(fin_buf.at[half], fin_r.at[half])
        for k in range(6):
            total = total + fin_buf[half, k].astype(F32)
        halves.append(total)

    gs = (ga, gb)

    def at_rows(half, px, py):
        p = py * NX + px if half else px * NY + py
        return gs[half].at[pl.ds(pl.multiple_of(p * ROWS, ROWS), ROWS), :]

    for half in range(2):
        at_rows(half, x, y)[...] = halves[half].astype(BF16)

    def ag_copy(half, via, p, q):
        blk = at_rows(half, *[(z + 4 - w) % 4 for z, w in zip((x, y), flip(half, via, 0))])
        n = half * 6 + ((0, 1, 2, 1)[p] if p == 0 or q else 2 + p)
        dev = seq_at(*flip(half, p - via, q))
        return remote(blk, blk, ag_s.at[half], ag_r.at[n], (dev, c))

    for p in ORDER:
        for half in range(2):
            ag_copy(half, 0, p, 0).start()
    first = c % 2 == 0

    def far(relayed):
        for p, q in ((1, 2), (3, 2), (2, 1), (2, 3)):
            for half in range(2):
                if not relayed:
                    ag_copy(half, 0, p, q).start()
                elif relayed == p:
                    ag_copy(half, p, p, q).start()

    for half in range(2):
        ag_copy(half, 0, 2, 2).start()
    pl.when(first)(lambda: far(0))
    for q in (2, 1, 3):
        for half in range(2):
            ag_copy(half, 0, 0, q).start()
    for d in ORDER:
        cnty_copy(d).start()
    for p in (1, 3):
        for half in range(2):
            ag_copy(half, 0, p, 0).wait_recv()
            for q in (1, 3):
                ag_copy(half, p, p, q).start()
        pl.when(jnp.logical_not(first))(lambda p=p: far(p))
    for half in range(2):
        ag_copy(half, 0, 2, 0).wait_recv()
    pl.when(jnp.logical_not(first))(lambda: far(2))
    wait_bytes(cnt_yb.at[pl.ds(1, 3)], cnt_r.at[1])
    tot = cnt_y[...] + cnt_yb[1] + cnt_yb[2] + cnt_yb[3]
    inv = 1.0 / jnp.maximum(tot, 1.0)
    inv_ref[...] = inv
    bias = jnp.where(tot > 0, jnp.log(1.0 + tot), F32(-1e9)).astype(BF16).astype(F32)
    bias_ref[...] = bias * LOG2E

    top = den = att = None
    for step, dists in ((0, (0,)), (2, (2,)), (1, (1, 3))):
        keys, rows = [], []
        for half in range(2):
            size = (3, 6, 3)[step] * ROWS
            wait_bytes(gs[half].at[pl.ds(0, size), :], ag_r.at[half * 6 + step])
        for d in dists:
            for half in range(2):
                g = (y + NY - d) % NY if half else (x + NX - d) % NX
                keys.append(gs[half][pl.ds(pl.multiple_of(g * MB, MB), MB), :])
                rows += [half * 8 + g * 2, half * 8 + g * 2 + 1]
        new = None
        for n, kb in enumerate(keys):
            raw = nt_dot(q2[...], kb)
            for j in range(2):
                r = rows[2 * n + j]
                t = raw[:, j * 128 : (j + 1) * 128] * inv_ref[pl.ds(r, 1), :]
                t = t + bias_ref[pl.ds(r, 1), :]
                sc[:, (2 * n + j) * 128 : (2 * n + j + 1) * 128] = t
                new = t if new is None else jnp.maximum(new, t)
        new = jnp.broadcast_to(jnp.max(new, axis=1, keepdims=True), (256, 128))
        if top is not None:
            new = jnp.maximum(top, new)
            alpha = jnp.exp2(top - new)
            den = den * alpha
            att = att * alpha
        top = new
        for n, kb in enumerate(keys):
            ps = []
            for j in range(2):
                r = rows[2 * n + j]
                e = jnp.exp2(sc[:, (2 * n + j) * 128 : (2 * n + j + 1) * 128] - top)
                den = e if den is None else den + e
                ps.append((e * inv_ref[pl.ds(r, 1), :]).astype(BF16))
            p = jnp.concatenate(ps, axis=1)
            pv = jnp.dot(p, kb, preferred_element_type=F32)
            att = pv if att is None else att + pv
    att = (att / jnp.sum(den, axis=1, keepdims=True)).astype(BF16)

    row = 0.0
    for k in range(2):
        part = slice(k * (HID // 2), (k + 1) * (HID // 2))
        hid = jnp.maximum(hc[part, :] + nt_dot(wt[part, D:], att), 0.0)
        hid = hid * jnp.concatenate([wcol[part, :], wcol[part, :]], axis=1)
        row = row + jnp.sum(hid, axis=0, keepdims=True)
    for j in range(NCAND):
        out_send[j, :, :32] = row[:, j * 32 : (j + 1) * 32]
    for j in range(1, NCAND):
        peer = (c + j) % NCAND
        remote(out_send.at[peer], out_buf.at[c], out_s.at[0], out_s.at[1], (s, peer)).start()
    out_buf[c] = out_send[c]
    wait_bytes(mine.at[pl.ds(0, 7)], cand_s.at[0])
    wait_bytes(cnt_xb.at[pl.ds(1, 3)], cnt_s.at[0])
    wait_bytes(cnt_yb.at[pl.ds(1, 3)], cnt_s.at[1])
    wait_bytes(add_buf, rs_s.at[0])
    wait_bytes(fin_buf, rs_s.at[1])
    for half in range(2):
        wait_bytes(gs[half].at[pl.ds(0, 15 * ROWS), :], ag_s.at[half])
    wait_bytes(out_buf.at[pl.ds(0, 7)], out_s.at[0])
    wait_bytes(out_buf.at[pl.ds(0, 7)], out_s.at[1])
    out_ref[...] = out_buf[:, 0, :32]


def on_device(
    behaviors, cluster_ids, lengths, candidates, w_query, w_key, w_hidden, b_hidden, w_out
):
    vmem = pl.BlockSpec(memory_space=pltpu.VMEM)
    dma = pltpu.SemaphoreType.DMA
    return pl.pallas_call(
        kernel,
        out_shape=pltpu.VMEM((8, 32), F32),
        in_specs=[pl.BlockSpec(memory_space=pltpu.HBM)] * 10,
        out_specs=vmem,
        scratch_shapes=[
            pltpu.SMEM((1, 1), jnp.int32),
            pltpu.VMEM((SLOTS, D), F32),
            pltpu.VMEM((1, SLOTS), jnp.int32),
            pltpu.VMEM((64, 128), jnp.int32),
            pltpu.VMEM((8, 32, D), BF16),
            pltpu.VMEM((D, D), BF16),
            pltpu.VMEM((D, D), BF16),
            pltpu.VMEM((2 * D, HID), BF16),
            pltpu.VMEM((1, HID), F32),
            pltpu.VMEM((1, HID), F32),
            pltpu.VMEM((2, SLOTS, D), BF16),
            pltpu.VMEM((16, SLOTS), BF16),
            pltpu.VMEM((16, SLOTS), BF16),
            pltpu.VMEM((2, 2 * ROWS, 2 * D), F32),
            pltpu.VMEM((ROWS, 2 * D), F32),
            pltpu.VMEM((2, 4, MB, D), BF16),
            pltpu.VMEM((2, 3, 3, ROWS, D), BF16),
            pltpu.VMEM((2, 3, ROWS, D), BF16),
            pltpu.VMEM((2, 6, ROWS, D), BF16),
            pltpu.VMEM((16, 128), F32),
            pltpu.VMEM((4, 16, 128), F32),
            pltpu.VMEM((16, 128), F32),
            pltpu.VMEM((4, 16, 128), F32),
            pltpu.VMEM((HALF, D), BF16),
            pltpu.VMEM((HALF, D), BF16),
            pltpu.VMEM((8, 32, D), BF16),
            pltpu.VMEM((256, D), BF16),
            pltpu.VMEM((HID, 2 * D), BF16),
            pltpu.VMEM((HID, 256), F32),
            pltpu.VMEM((HID, 128), F32),
            pltpu.VMEM((HID, 128), F32),
            pltpu.VMEM((8, 1, 128), F32),
            pltpu.VMEM((8, 1, 128), F32),
            pltpu.VMEM((16, 128), F32),
            pltpu.VMEM((16, 128), F32),
            pltpu.VMEM((256, 1024), F32),
            dma((CHUNKS,)),
            dma((9,)),
            dma((2,)),
            dma((2,)),
            dma((2,)),
            dma((2,)),
            dma((6,)),
            dma((2,)),
            dma((2,)),
            dma((12,)),
            dma((2,)),
        ],
        compiler_params=pltpu.CompilerParams(collective_id=0, has_side_effects=True),
        name="fused",
    )(
        lengths,
        behaviors,
        cluster_ids,
        cluster_ids.reshape(64, 128),
        candidates,
        w_query,
        w_key,
        w_hidden,
        b_hidden.reshape(1, HID),
        w_out.reshape(1, HID),
    )


def solution(mesh):
    in_specs = (
        P("cand", "seq", None),
        P("cand", "seq"),
        P("cand", "seq"),
        P(None, ("seq", "cand"), None),
        P(),
        P(),
        P(),
        P(),
        P(),
    )
    return jax.shard_map(
        on_device,
        mesh=mesh,
        in_specs=in_specs,
        out_specs=P(None, ("seq", "cand")),
        check_vma=False,
    )
```
